32 devices in a mesh: pb: 8 (over y, x, core), ka: 4 (over z).
Axes of the slice: x: 2, y: 2, z: 4, core: 2. Of those that a mesh axis runs over, the one named last changes fastest.
Arguments:
- queries: bfloat16 [4096, 1024], P(('pb', 'ka')), may hold values from -200 to 200
- keys: bfloat16 [4096, 128], P(('pb', 'ka')), may hold values from -6 to 6
- values: bfloat16 [4096, 128], P(('pb', 'ka')), may hold values from -6 to 6
- positions: int32 [4096], replicated, may hold values from 0 to 4095, as said below
Outputs:
- attended: float32 [4096, 1024], P(('pb', 'ka'))
The draws below stay inside these ranges and needn't reach their ends.
Inputs may be any that keep to these rules, and one draw needn't show every extreme that they name: A permutation of 0 to 4095; each aligned run of 128 slots holds consecutive positions in increasing order.
All inputs are finite; a program needn't handle non-finite values.
Results may differ from the reference program's by a relative error of at most 0.0003.
Values may be sent and summed in bfloat16 or wider, within the bound.
No kernel may reach another device: no remote copies, remote signals or barrier semaphores. Data moves between devices by JAX's collectives and lax.ppermute only.
A program may use at most 64 MiB of HBM per device.

```python
import jax
import jax.numpy as jnp
from jax import lax

HD = 128
H = 8
TOK_DEV = 128
SEQ = 4096


def joint_draw(key):
    base = jax.random.fold_in(key, 11)
    key_query, key_key, key_pos = jax.random.split(base, 3)
    runs = SEQ // TOK_DEV
    order = jax.random.permutation(key_pos, runs).astype(jnp.int32)
    positions = (order[:, None] * TOK_DEV + jnp.arange(TOK_DEV, dtype=jnp.int32)[None, :]).reshape(-1)
    keys = jnp.clip(jax.random.normal(key_key, (SEQ, HD), jnp.float32), -6.0, 6.0)
    queries = jnp.clip(jax.random.normal(key_query, (SEQ, H * HD), jnp.float32), -6.0, 6.0)
    return (queries, keys, positions)


def draw_queries(key, part):
    return joint_draw(key)[0].astype(jnp.bfloat16)


def draw_keys(key, part):
    return joint_draw(key)[1].astype(jnp.bfloat16)


def draw_positions(key, part):
    return joint_draw(key)[2]


def level_of(own_key, shape, cuts, least, high):
    gain = 1.0
    for dim, blocks in cuts:
        draws = jax.random.uniform(jax.random.fold_in(jax.random.fold_in(own_key, 6), dim), (blocks,), jnp.float32, least / len(cuts), high / len(cuts))
        gain = gain * jnp.repeat(jnp.exp(draws), shape[dim] // blocks).reshape((-1,) + (1,) * (len(shape) - 1 - dim))
    return gain


def centred(key, dims, deviation, limit, pieces=(), held_as=jnp.bfloat16):
    result = deviation * jax.random.normal(key, dims, jnp.float32)
    if pieces:
        result = result * level_of(key, dims, pieces, -0.22, 0.18)
    return jnp.clip(result, -limit, limit).astype(held_as)


def setup_inputs(seed: int = 0) -> dict:
    splits = jax.random.split(jax.random.key(seed), 5)
    return {
        "queries": draw_queries(jax.random.fold_in(splits[4], 71), 0),
        "keys": draw_keys(jax.random.fold_in(splits[4], 71), 0),
        "values": centred(splits[2], (SEQ, HD), 1.0, 6.0, ((0, 32),)),
        "positions": draw_positions(jax.random.fold_in(splits[4], 71), 0),
    }


def reference(queries, keys, values, positions):
    total_rows = queries.shape[0]
    block = min(128, total_rows)
    scale = 1.0 / (HD ** 0.5)
    keys_wide = keys.astype(jnp.float32)
    values_wide = values.astype(jnp.float32)

    def one_block(index):
        rows = lax.dynamic_slice_in_dim(queries, index * block, block, 0).astype(jnp.float32).reshape(block, H, HD)
        row_pos = lax.dynamic_slice_in_dim(positions, index * block, block, 0)
        score = jnp.einsum("qhd,kd->hqk", rows, keys_wide, precision=lax.Precision.HIGHEST) * scale
        visible = positions[None, None, :] <= row_pos[None, :, None]
        masked = jnp.where(visible, score, jnp.float32(-1e30))
        top = jnp.max(masked, axis=-1, keepdims=True)
        prob = jnp.where(visible, jnp.exp(masked - top), jnp.float32(0.0))
        total = jnp.sum(prob, axis=-1)
        output = jnp.einsum("hqk,kd->hqd", prob, values_wide, precision=lax.Precision.HIGHEST)
        output = output / total[:, :, None]
        return jnp.transpose(output, (1, 0, 2)).reshape(block, H * HD)

    blocks = lax.map(one_block, jnp.arange(total_rows // block, dtype=jnp.int32))
    return blocks.reshape(total_rows, H * HD)
```

```python
import functools
import math

import jax
import jax.numpy as jnp
from jax import lax
from jax.experimental import pallas as pl
from jax.experimental.pallas import tpu as pltpu
from jax.sharding import PartitionSpec as P

HD = 128
AXES = ("pb", "ka")
BIG = -1e30
STEP = 4

VMEM = pl.BlockSpec(memory_space=pltpu.VMEM)
SMEM = pl.BlockSpec(memory_space=pltpu.SMEM)


def combine(rows, keys, values, largest, totals, summed, to_log2, mask=None):
    score = lax.dot_general(
        rows, keys, (((1,), (1,)), ((), ())), preferred_element_type=jnp.float32
    )
    if mask is not None:
        score = jnp.where(mask, score, BIG)
    parts = [score[:, at : at + HD] for at in range(0, keys.shape[0], HD)]
    top = jnp.max(functools.reduce(jnp.maximum, parts), axis=1, keepdims=True)
    if largest is None:
        top = jnp.broadcast_to(top, (rows.shape[0], HD))
    else:
        top = jnp.maximum(largest, top)
    weights = [jnp.exp2((part - top) * to_log2) for part in parts]
    if mask is not None:
        weights = [jnp.where(mask, weight, 0.0) for weight in weights]
    total = functools.reduce(jnp.add, weights)
    weight = jnp.concatenate(weights, axis=1) if len(weights) > 1 else weights[0]
    high = weight.astype(jnp.bfloat16)
    low = (weight - high.astype(jnp.float32)).astype(jnp.bfloat16)
    over = (((1,), (0,)), ((), ()))
    result = lax.dot_general(high, values, over, preferred_element_type=jnp.float32)
    result += lax.dot_general(low, values, over, preferred_element_type=jnp.float32)
    if largest is None:
        return top, total, result
    factor = jnp.exp2((largest - top) * to_log2)
    return top, totals * factor + total, summed * factor + result


def attend_kernel(masks, first, last, size_key, token, *refs):
    count = len(masks)
    starts_ref, queries_ref = refs[:2]
    block_refs = refs[2 : 2 + count]
    rest = refs[2 + count :]
    state_in, rest = (None, rest) if first else (rest[:3], rest[3:])
    outs, (rows_ref, order_ref), state = (
        (rest[:1], rest[1:3], rest[3:6]) if last else (rest[:3], rest[3:5], rest[:3])
    )
    heads = queries_ref.shape[1] // HD
    to_log2 = math.log2(math.e) / HD**0.5
    own_pb, own_ka = lax.axis_index("pb"), lax.axis_index("ka")
    own_start = starts_ref[own_pb * size_key + own_ka]
    for head in range(heads):
        rows_ref[head * token : (head + 1) * token, :] = queries_ref[:, head * HD : (head + 1) * HD]

    def pieces(ref, places):
        offsets = [pl.multiple_of(place * 2 * token, 2 * token) for place in places]
        keys = [ref[pl.ds(offset, token), :] for offset in offsets]
        values = [ref[pl.ds(offset + token, token), :] for offset in offsets]
        if len(places) == 1:
            return keys[0], values[0]
        return jnp.concatenate(keys, axis=0), jnp.concatenate(values, axis=0)

    def update(ref, places):
        keys, values = pieces(ref, places)
        new = combine(
            rows_ref[...], keys, values, state[0][...], state[1][...], state[2][...], to_log2
        )
        for held, value in zip(state, new):
            held[...] = value

    if first:
        shape = (heads, token, token)
        causal = lax.broadcasted_iota(jnp.int32, shape, 2) <= lax.broadcasted_iota(
            jnp.int32, shape, 1
        )
        keys, values = pieces(block_refs[0], [0])
        new = combine(
            rows_ref[...],
            keys,
            values,
            None,
            None,
            None,
            to_log2,
            causal.reshape(heads * token, token),
        )
        for held, value in zip(state, new):
            held[...] = value
    elif last:
        for held, value in zip(state, state_in):
            held[...] = value[...]
    else:
        for held, value in zip(state, state_in):
            held[...] = value[...]

    core = own_pb % 2
    for ref, (mask_even, mask_odd) in zip(block_refs, masks):
        source = own_pb ^ jnp.where(core == 0, mask_even, mask_odd)

        def note(place, seen):
            start = starts_ref[source * size_key + (own_ka ^ place)]
            visible = start < own_start

            @pl.when(visible)
            def _():
                order_ref[seen] = place

            return seen + visible.astype(jnp.int32)

        seen = lax.fori_loop(0, size_key, note, jnp.int32(0))

        def many(index, _):
            update(ref, [order_ref[index * STEP + at] for at in range(STEP)])
            return 0

        lax.fori_loop(0, seen // STEP, many, 0)
        left = seen % STEP
        done = seen - left
        width = STEP // 2
        while width:

            @pl.when((left & width) != 0)
            def _():
                base = done + (left & ~(2 * width - 1))
                update(ref, [order_ref[base + at] for at in range(width)])

            width //= 2

    if last:
        (out_ref,) = outs
        for head in range(heads):
            rows = slice(head * token, (head + 1) * token)
            total = jnp.sum(state[1][rows, :], axis=1, keepdims=True)
            out_ref[:, head * HD : (head + 1) * HD] = state[2][rows, :] / total


def attend(starts, queries, blocks, state, size_key, last):
    token, width = queries.shape
    rows = width // HD * token
    buffers, masks = zip(*blocks)
    sums = [jax.ShapeDtypeStruct((rows, HD), jnp.float32)] * 3
    scratch = [pltpu.VMEM((rows, HD), jnp.bfloat16), pltpu.SMEM((size_key,), jnp.int32)]
    if last:
        scratch += [pltpu.VMEM((rows, HD), jnp.float32)] * 3
    kernel = functools.partial(attend_kernel, masks, state is None, last, size_key, token)
    operands = [starts, queries, *buffers, *(state or ())]
    result = pl.pallas_call(
        kernel,
        out_shape=[jax.ShapeDtypeStruct((token, width), jnp.float32)] if last else sums,
        in_specs=[SMEM] + [VMEM] * (len(operands) - 1),
        out_specs=[VMEM] if last else [VMEM] * 3,
        scratch_shapes=scratch,
    )(*operands)
    return result[0] if last else tuple(result)


def move(array, mask_even, mask_odd, place=0):
    size_query, size_key = lax.axis_size("pb"), lax.axis_size("ka")
    pairs = []
    for query in range(size_query):
        source = query ^ (mask_odd if query % 2 else mask_even)
        for key in range(size_key):
            pairs.append((source * size_key + (key ^ place), query * size_key + key))
    return lax.ppermute(array, AXES, pairs)


def on_device(queries, keys, values, positions):
    token = queries.shape[0]
    size_query, size_key = lax.axis_size("pb"), lax.axis_size("ka")
    assert size_query & (size_query - 1) == 0 and size_key & (size_key - 1) == 0
    starts = positions.reshape(-1, token)[:, 0]
    own = jnp.concatenate([keys, values], axis=0)
    column = jnp.concatenate([own] + [move(own, 0, 0, place) for place in range(1, size_key)], axis=0)

    bits = [1 << at for at in range(1, size_query.bit_length() - 1)]
    held = [(column, (0, 0))]
    groups = [[held[0]]]
    while bits:
        one, two, bits = bits[0], (bits[1] if len(bits) > 1 else None), bits[2:]
        near, far = [], []
        for array, (even, odd) in held:
            if two is None:
                near.append((move(array, one, one), (even ^ one, odd ^ one)))
                continue
            first = move(array, one, two)
            near.append((first, (even ^ one, odd ^ two)))
            near.append((move(array, two, one), (even ^ two, odd ^ one)))
            far.append((move(first, two, one), (even ^ one ^ two, odd ^ one ^ two)))
        held += near + far
        groups += [group for group in (near, far) if group]

    state = None
    for at, group in enumerate(groups):
        blocks = []
        for array, (even, odd) in group:
            blocks.append((array, (even, odd)))
            blocks.append((move(array, 1, 1), (1 ^ odd, 1 ^ even)))
        state = attend(starts, queries, blocks, state, size_key, at == len(groups) - 1)
    return state


def solution(mesh):
    return jax.shard_map(
        on_device,
        mesh=mesh,
        in_specs=(P(AXES, None), P(AXES, None), P(AXES, None), P()),
        out_specs=P(AXES, None),
        check_vma=False,
    )
```

```python
import functools
import math

import jax
import jax.numpy as jnp
from jax import lax
from jax.experimental import pallas as pl
from jax.experimental.pallas import tpu as pltpu
from jax.sharding import PartitionSpec as P


HD = 128
AXES = ("pb", "ka")
BIG = -1e30
STEP = 4
LIMIT = 24 << 20

VMEM = pl.BlockSpec(memory_space=pltpu.VMEM)
SMEM = pl.BlockSpec(memory_space=pltpu.SMEM)


def combine(rows, keys, values, largest, totals, summed, to_log2, mask=None):
    score = lax.dot_general(
        rows, keys, (((1,), (1,)), ((), ())), preferred_element_type=jnp.float32
    )
    if mask is not None:
        score = jnp.where(mask, score, BIG)
    parts = [score[:, at : at + HD] for at in range(0, keys.shape[0], HD)]
    top = jnp.max(functools.reduce(jnp.maximum, parts), axis=1, keepdims=True)
    if largest is None:
        top = jnp.broadcast_to(top, (rows.shape[0], HD))
    else:
        top = jnp.maximum(largest, top)
    weights = [jnp.exp2((part - top) * to_log2) for part in parts]
    if mask is not None:
        weights = [jnp.where(mask, weight, 0.0) for weight in weights]
    total = functools.reduce(jnp.add, weights)
    weight = jnp.concatenate(weights, axis=1) if len(weights) > 1 else weights[0]
    high = weight.astype(jnp.bfloat16)
    low = (weight - high.astype(jnp.float32)).astype(jnp.bfloat16)
    over = (((1,), (0,)), ((), ()))
    result = lax.dot_general(high, values, over, preferred_element_type=jnp.float32)
    result += lax.dot_general(low, values, over, preferred_element_type=jnp.float32)
    if largest is None:
        return top, total, result
    factor = jnp.exp2((largest - top) * to_log2)
    return top, totals * factor + total, summed * factor + result


def attend_kernel(masks, first, last, size_key, token, *refs):
    count = len(masks)
    queries_ref = refs[0]
    block_refs = refs[1 : 1 + count]
    rest = refs[1 + count :]
    if not first:
        starts_ref, rest = rest[0], rest[1:]
    state_in, rest = (None, rest) if first else (rest[:3], rest[3:])
    outs, (rows_ref, order_ref), state = (
        (rest[:1], rest[1:3], rest[3:6]) if last else (rest[:3], rest[3:5], rest[:3])
    )
    heads = queries_ref.shape[1] // HD
    to_log2 = math.log2(math.e) / HD**0.5
    for head in range(heads):
        rows_ref[head * token : (head + 1) * token, :] = queries_ref[:, head * HD : (head + 1) * HD]

    def pieces(ref, places):
        offsets = [pl.multiple_of(place * 2 * token, 2 * token) for place in places]
        keys = [ref[pl.ds(offset, token), :] for offset in offsets]
        values = [ref[pl.ds(offset + token, token), :] for offset in offsets]
        if len(places) == 1:
            return keys[0], values[0]
        return jnp.concatenate(keys, axis=0), jnp.concatenate(values, axis=0)

    def update(ref, places):
        keys, values = pieces(ref, places)
        new = combine(
            rows_ref[...], keys, values, state[0][...], state[1][...], state[2][...], to_log2
        )
        for held, value in zip(state, new):
            held[...] = value

    if first:
        shape = (heads, token, token)
        causal = lax.broadcasted_iota(jnp.int32, shape, 2) <= lax.broadcasted_iota(
            jnp.int32, shape, 1
        )
        keys, values = pieces(block_refs[0], [0])
        new = combine(
            rows_ref[...],
            keys,
            values,
            None,
            None,
            None,
            to_log2,
            causal.reshape(heads * token, token),
        )
        for held, value in zip(state, new):
            held[...] = value
        return
    for held, value in zip(state, state_in):
        held[...] = value[...]

    own_pb, own_ka = lax.axis_index("pb"), lax.axis_index("ka")
    own_start = starts_ref[own_pb * size_key + own_ka]
    core = own_pb % 2
    for ref, (mask_even, mask_odd) in zip(block_refs, masks):
        source = own_pb ^ jnp.where(core == 0, mask_even, mask_odd)

        def note(place, seen):
            start = starts_ref[source * size_key + (own_ka ^ place)]
            visible = start < own_start

            @pl.when(visible)
            def _():
                order_ref[seen] = place

            return seen + visible.astype(jnp.int32)

        seen = lax.fori_loop(0, size_key, note, jnp.int32(0))

        def many(index, _):
            update(ref, [order_ref[index * STEP + at] for at in range(STEP)])
            return 0

        lax.fori_loop(0, seen // STEP, many, 0)
        left = seen % STEP
        done = seen - left
        width = STEP // 2
        while width:

            @pl.when((left & width) != 0)
            def _():
                base = done + (left & ~(2 * width - 1))
                update(ref, [order_ref[base + at] for at in range(width)])

            width //= 2

    if last:
        (out_ref,) = outs
        for head in range(heads):
            rows = slice(head * token, (head + 1) * token)
            total = jnp.sum(state[1][rows, :], axis=1, keepdims=True)
            out_ref[:, head * HD : (head + 1) * HD] = state[2][rows, :] / total


def attend(starts, queries, blocks, state, size_key, last):
    token, width = queries.shape
    rows = width // HD * token
    buffers, masks = zip(*blocks)
    sums = [jax.ShapeDtypeStruct((rows, HD), jnp.float32)] * 3
    scratch = [pltpu.VMEM((rows, HD), jnp.bfloat16), pltpu.SMEM((size_key,), jnp.int32)]
    if last:
        scratch += [pltpu.VMEM((rows, HD), jnp.float32)] * 3
    kernel = functools.partial(attend_kernel, masks, state is None, last, size_key, token)
    operands = [queries, *buffers] + ([starts, *state] if state else [])
    result = pl.pallas_call(
        kernel,
        out_shape=[jax.ShapeDtypeStruct((token, width), jnp.float32)] if last else sums,
        in_specs=[SMEM if operand is starts else VMEM for operand in operands],
        out_specs=[VMEM] if last else [VMEM] * 3,
        scratch_shapes=scratch,
        compiler_params=pltpu.CompilerParams(vmem_limit_bytes=LIMIT),
        cost_estimate=pl.CostEstimate(
            flops=6 * rows * HD * token * size_key * len(buffers),
            transcendentals=rows * token * size_key * len(buffers),
            bytes_accessed=1 << 20,
        ),
    )(*operands)
    return result[0] if last else tuple(result)


def move(array, mask_even, mask_odd, place):
    size_query, size_key = lax.axis_size("pb"), lax.axis_size("ka")
    pairs = []
    for query in range(size_query):
        source = query ^ (mask_odd if query % 2 else mask_even)
        for key in range(size_key):
            pairs.append((source * size_key + (key ^ place), query * size_key + key))
    return lax.ppermute(array, AXES, pairs)


def stages(size_query):
    bits = [1 << at for at in range(1, size_query.bit_length() - 1)]
    return [bits[at : at + 2] for at in range(0, len(bits), 2)]


def swap(item):
    array, (even, odd) = item
    return move(array, 1, 1, 0), (1 ^ odd, 1 ^ even)


def gathered_attention(queries, keys, values, positions):
    token = queries.shape[0]
    size_query, size_key = lax.axis_size("pb"), lax.axis_size("ka")
    assert size_query & (size_query - 1) == 0 and size_key & (size_key - 1) == 0
    starts = positions.reshape(-1, token)[:, 0]
    own = jnp.concatenate([keys, values], axis=0)
    others = [move(own, 0, 0, place) for place in range(1, size_key)]
    column = jnp.concatenate([own] + others, axis=0)

    held = [(column, (0, 0))]
    groups = [[(own, (0, 0))], [held[0], swap(held[0])]]
    for bits in stages(size_query):
        one, two = bits[0], bits[-1]
        near, far = [], []
        for array, (even, odd) in held:
            first = move(array, one, two, 0)
            near.append((first, (even ^ one, odd ^ two)))
            if one != two:
                second = move(array, two, one, 0)
                near.append((second, (even ^ two, odd ^ one)))
                both = one ^ two
                far.append((move(first, two, one, 0), (even ^ both, odd ^ both)))
        held += near + far
        swapped = [swap(item) for item in near]
        groups.append(near)
        groups.append(swapped + far)
        if far:
            groups.append([swap(item) for item in far])

    state = None
    for at, group in enumerate(groups):
        state = attend(starts, queries, group, state, size_key, at == len(groups) - 1)
    return state


def solution(mesh):
    return jax.shard_map(
        gathered_attention,
        mesh=mesh,
        in_specs=(P(AXES, None), P(AXES, None), P(AXES, None), P()),
        out_specs=P(AXES, None),
        check_vma=False,
    )
```

```python
import functools
import math

import jax
import jax.numpy as jnp
from jax import lax
from jax.experimental import pallas as pl
from jax.experimental.pallas import tpu as pltpu
from jax.sharding import PartitionSpec as P


HD = 128
AXES = ("pb", "ka")
BIG = -1e30
STEP = 4
LIMIT = 24 << 20

VMEM = pl.BlockSpec(memory_space=pltpu.VMEM)
SMEM = pl.BlockSpec(memory_space=pltpu.SMEM)


def combine(rows, keys, values, sums, to_log2, mask=None):
    score = lax.dot_general(
        rows, keys, (((1,), (1,)), ((), ())), preferred_element_type=jnp.float32
    )
    if mask is not None:
        score = jnp.where(mask, score, BIG)
    parts = [score[:, at : at + HD] for at in range(0, keys.shape[0], HD)]
    top = jnp.max(functools.reduce(jnp.maximum, parts), axis=1, keepdims=True)
    if sums is None:
        top = jnp.broadcast_to(top, (rows.shape[0], HD))
    else:
        top = jnp.maximum(sums[0], top)
    weights = [jnp.exp2((part - top) * to_log2) for part in parts]
    if mask is not None:
        weights = [jnp.where(mask, weight, 0.0) for weight in weights]
    total = functools.reduce(jnp.add, weights)
    weight = jnp.concatenate(weights, axis=1) if len(weights) > 1 else weights[0]
    high = weight.astype(jnp.bfloat16)
    low = (weight - high.astype(jnp.float32)).astype(jnp.bfloat16)
    over = (((1,), (0,)), ((), ()))
    result = lax.dot_general(high, values, over, preferred_element_type=jnp.float32)
    result += lax.dot_general(low, values, over, preferred_element_type=jnp.float32)
    if sums is None:
        return top, total, result
    largest, totals, summed = sums
    factor = jnp.exp2((largest - top) * to_log2)
    return top, totals * factor + total, summed * factor + result


TO_LOG2 = math.log2(math.e) / HD**0.5


def own_kernel(queries_ref, own_ref, rows_ref, largest_ref, totals_ref, summed_ref):
    token, width = queries_ref.shape
    heads = width // HD
    for head in range(heads):
        rows_ref[head * token : (head + 1) * token, :] = queries_ref[:, head * HD : (head + 1) * HD]
    shape = (heads, token, token)
    causal = lax.broadcasted_iota(jnp.int32, shape, 2) <= lax.broadcasted_iota(jnp.int32, shape, 1)
    keys, values = own_ref[:token, :], own_ref[token:, :]
    mask = causal.reshape(heads * token, token)
    new = combine(rows_ref[...], keys, values, None, TO_LOG2, mask)
    for held, value in zip((largest_ref, totals_ref, summed_ref), new):
        held[...] = value


def attend_kernel(pieces, last, size_key, token, *refs):
    count = len(pieces)
    starts_ref, rows_ref = refs[:2]
    block_refs = refs[2 : 2 + count]
    outs, (keys_ref, values_ref) = refs[5 + count : -2], refs[-2:]
    state = outs[:3]
    own_pb, own_ka = lax.axis_index("pb"), lax.axis_index("ka")
    own_start = starts_ref[own_pb * size_key + own_ka]
    core = own_pb % 2

    seen = jnp.int32(0)
    for ref, (base, mask_even, mask_odd) in zip(block_refs, pieces):
        source = (own_pb ^ jnp.where(core == 0, mask_even, mask_odd)) * size_key

        def note(at, seen):
            visible = starts_ref[source + (own_ka ^ (base + at))] < own_start

            @pl.when(visible)
            def _():
                target = pl.ds(pl.multiple_of(seen * token, token), token)
                offset = pl.multiple_of(at * 2 * token, token)
                keys_ref[target, :] = ref[pl.ds(offset, token), :]
                values_ref[target, :] = ref[pl.ds(offset + token, token), :]

            return seen + visible.astype(jnp.int32)

        seen = lax.fori_loop(0, ref.shape[0] // (2 * token), note, seen)

    def update(first, number):
        part = pl.ds(pl.multiple_of(first * token, token), number * token)
        sums = [held[...] for held in state]
        new = combine(rows_ref[...], keys_ref[part, :], values_ref[part, :], sums, TO_LOG2)
        for held, value in zip(state, new):
            held[...] = value

    def many(index, _):
        update(index * STEP, STEP)
        return 0

    lax.fori_loop(0, seen // STEP, many, 0)
    left = seen % STEP
    done = seen - left
    number = STEP // 2
    while number:
        pl.when((left & number) != 0)(
            functools.partial(update, done + (left & ~(2 * number - 1)), number)
        )
        number //= 2

    if last:
        out_ref = outs[3]
        for head in range(out_ref.shape[1] // HD):
            rows = slice(head * token, (head + 1) * token)
            total = jnp.sum(state[1][rows, :], axis=1, keepdims=True)
            out_ref[:, head * HD : (head + 1) * HD] = state[2][rows, :] / total


def params(rows, token, blocks):
    return dict(
        compiler_params=pltpu.CompilerParams(vmem_limit_bytes=LIMIT),
        cost_estimate=pl.CostEstimate(
            flops=6 * rows * HD * token * blocks,
            transcendentals=rows * token * blocks,
            bytes_accessed=1 << 20,
        ),
    )


def attend_own(queries, own):
    token, width = queries.shape
    rows = width // HD * token
    sums = jax.ShapeDtypeStruct((rows, HD), jnp.float32)
    return pl.pallas_call(
        own_kernel,
        out_shape=[jax.ShapeDtypeStruct((rows, HD), jnp.bfloat16), sums, sums, sums],
        in_specs=[VMEM] * 2,
        out_specs=[VMEM] * 4,
        **params(rows, token, 1),
    )(queries, own)


def attend(starts, state, items, size_key, shape, last):
    token, width = shape
    rows = width // HD * token
    arrays, pieces = zip(*items)
    blocks = sum(array.shape[0] for array in arrays) // (2 * token)
    outs = [jax.ShapeDtypeStruct((rows, HD), jnp.float32)] * 3
    if last:
        outs.append(jax.ShapeDtypeStruct(shape, jnp.float32))
    operands = [starts, state[0], *arrays, *state[1:]]
    result = pl.pallas_call(
        functools.partial(attend_kernel, pieces, last, size_key, token),
        out_shape=outs,
        in_specs=[SMEM] + [VMEM] * (len(operands) - 1),
        out_specs=[VMEM] * len(outs),
        input_output_aliases={2 + len(arrays) + at: at for at in range(3)},
        scratch_shapes=[pltpu.VMEM((blocks * token, HD), jnp.bfloat16)] * 2,
        **params(rows, token, blocks),
    )(*operands)
    return result[3] if last else (state[0], *result)


def move(array, mask_even, mask_odd, place):
    size_query, size_key = lax.axis_size("pb"), lax.axis_size("ka")
    pairs = []
    for query in range(size_query):
        source = query ^ (mask_odd if query % 2 else mask_even)
        for key in range(size_key):
            pairs.append((source * size_key + (key ^ place), query * size_key + key))
    return lax.ppermute(array, AXES, pairs)


def stages(size_query):
    bits = [1 << at for at in range(1, size_query.bit_length() - 1)]
    return [bits[at : at + 2] for at in range(0, len(bits), 2)]


def paired(size_query, size_key):
    plan = stages(size_query)
    return len(plan) == 1 and len(plan[0]) == 2 and size_key > 1


def swap(item):
    array, (base, even, odd) = item
    return move(array, 1, 1, 0), (base, 1 ^ odd, 1 ^ even)


def spread(item, bits):
    array, (base, even, odd) = item
    one, two = bits[0], bits[-1]
    first = move(array, one, two, 0)
    near = [(first, (base, even ^ one, odd ^ two))]
    if one == two:
        return near, []
    second = move(array, two, one, 0)
    near.append((second, (base, even ^ two, odd ^ one)))
    both = one ^ two
    third = move(first, two, one, 0)
    return near, [(third, (base, even ^ both, odd ^ both))]


def gathered_attention(queries, keys, values, positions):
    token = queries.shape[0]
    size_query, size_key = lax.axis_size("pb"), lax.axis_size("ka")
    assert size_query & (size_query - 1) == 0 and size_key & (size_key - 1) == 0
    starts = positions.reshape(-1, token)[:, 0]
    own = jnp.concatenate([keys, values], axis=0)
    column = [own] + [move(own, 0, 0, place) for place in range(1, size_key)]
    half = max(size_key // 2, 1)
    held = [
        (jnp.concatenate(column[base : base + half], axis=0), (base, 0, 0))
        for base in range(0, size_key, half)
    ]

    state = attend_own(queries, own)
    groups = []
    plan = stages(size_query)
    if paired(size_query, size_key):
        (lower, upper), bits = held, plan[0]
        near, far = spread(lower, bits)
        near_up, far_up = spread(upper, bits)
        groups.append([lower, swap(lower)])
        groups.append(near + [swap(item) for item in near])
        groups.append([upper, swap(upper)] + far + [swap(item) for item in far])
        groups.append(near_up)
        groups.append([swap(item) for item in near_up] + far_up)
        groups.append([swap(item) for item in far_up])
    else:
        groups.append(held + [swap(item) for item in held])
        for bits in plan:
            near, far = [], []
            for item in held:
                more_near, more_far = spread(item, bits)
                near += more_near
                far += more_far
            groups.append(near)
            groups.append([swap(item) for item in near] + far)
            if far:
                groups.append([swap(item) for item in far])
            held += near + far

    for at, group in enumerate(groups):
        state = attend(starts, state, group, size_key, queries.shape, at == len(groups) - 1)
    return state


def solution(mesh):
    return jax.shard_map(
        gathered_attention,
        mesh=mesh,
        in_specs=(P(AXES, None), P(AXES, None), P(AXES, None), P()),
        out_specs=P(AXES, None),
        check_vma=False,
    )
```

```python
import functools
import math

import jax
import jax.numpy as jnp
from jax import lax
from jax.experimental import pallas as pl
from jax.experimental.pallas import tpu as pltpu
from jax.sharding import PartitionSpec as P


HD = 128
AXES = ("pb", "ka")
BIG = -1e30
STEP = 4
LIMIT = 24 << 20

VMEM = pl.BlockSpec(memory_space=pltpu.VMEM)
SMEM = pl.BlockSpec(memory_space=pltpu.SMEM)


def combine(rows, keys, values, sums, to_log2, mask=None):
    score = lax.dot_general(
        rows, keys, (((1,), (1,)), ((), ())), preferred_element_type=jnp.float32
    )
    if mask is not None:
        score = jnp.where(mask, score, BIG)
    parts = [score[:, at : at + HD] for at in range(0, keys.shape[0], HD)]
    top = jnp.max(functools.reduce(jnp.maximum, parts), axis=1, keepdims=True)
    if sums is None:
        top = jnp.broadcast_to(top, (rows.shape[0], HD))
    else:
        top = jnp.maximum(sums[0], top)
    weights = [jnp.exp2((part - top) * to_log2) for part in parts]
    if mask is not None:
        weights = [jnp.where(mask, weight, 0.0) for weight in weights]
    total = functools.reduce(jnp.add, weights)
    weight = jnp.concatenate(weights, axis=1) if len(weights) > 1 else weights[0]
    high = weight.astype(jnp.bfloat16)
    low = (weight - high.astype(jnp.float32)).astype(jnp.bfloat16)
    over = (((1,), (0,)), ((), ()))
    result = lax.dot_general(high, values, over, preferred_element_type=jnp.float32)
    result += lax.dot_general(low, values, over, preferred_element_type=jnp.float32)
    if sums is None:
        return top, total, result
    largest, totals, summed = sums
    factor = jnp.exp2((largest - top) * to_log2)
    return top, totals * factor + total, summed * factor + result


TO_LOG2 = math.log2(math.e) / HD**0.5


def own_kernel(queries_ref, own_ref, rows_ref, largest_ref, totals_ref, summed_ref):
    token, width = queries_ref.shape
    heads = width // HD
    for head in range(heads):
        rows_ref[head * token : (head + 1) * token, :] = queries_ref[:, head * HD : (head + 1) * HD]
    shape = (heads, token, token)
    causal = lax.broadcasted_iota(jnp.int32, shape, 2) <= lax.broadcasted_iota(jnp.int32, shape, 1)
    keys, values = own_ref[:token, :], own_ref[token:, :]
    mask = causal.reshape(heads * token, token)
    new = combine(rows_ref[...], keys, values, None, TO_LOG2, mask)
    for held, value in zip((largest_ref, totals_ref, summed_ref), new):
        held[...] = value


def attend_kernel(pieces, groups, fresh, pack, size_key, token, *refs):
    refs = list(refs)
    take = lambda number: [refs.pop(0) for _ in range(number)]
    (starts_ref,) = take(1)
    rows_refs = take(len(groups))
    block_refs = take(len(pieces))
    take(3 * (len(groups) - len(fresh)))
    states = [take(3) for _ in groups]
    packed_refs = take(1 if pack else 0)
    keys_ref, values_ref = take(2)

    own_pb, own_ka = lax.axis_index("pb"), lax.axis_index("ka")
    core = own_pb % 2
    bounds = [starts_ref[(own_pb ^ group) * size_key + own_ka] for group in groups]
    low = functools.reduce(jnp.minimum, bounds)
    high = functools.reduce(jnp.maximum, bounds)

    def compact(seen, inside):
        for ref, parts in zip(block_refs, pieces):
            for offset, number, base, mask_even, mask_odd in parts:
                source = (own_pb ^ jnp.where(core == 0, mask_even, mask_odd)) * size_key
                for at in range(number):
                    visible = inside(starts_ref[source + (own_ka ^ (base + at))])
                    row = (offset + at) * 2 * token

                    @pl.when(visible)
                    def _():
                        target = pl.ds(pl.multiple_of(seen * token, token), token)
                        keys_ref[target, :] = ref[row : row + token, :]
                        values_ref[target, :] = ref[row + token : row + 2 * token, :]

                    seen = seen + visible.astype(jnp.int32)
        return seen

    both = compact(jnp.int32(0), lambda start: start < low)
    some = both
    if len(groups) > 1:
        some = compact(both, lambda start: (start >= low) & (start < high))

    def attend_group(rows_ref, state, seen):
        def update(first, number):
            part = pl.ds(pl.multiple_of(first * token, token), number * token)
            sums = [held[...] for held in state]
            new = combine(rows_ref[...], keys_ref[part, :], values_ref[part, :], sums, TO_LOG2)
            for held, value in zip(state, new):
                held[...] = value

        def many(index, _):
            update(index * STEP, STEP)
            return 0

        lax.fori_loop(0, seen // STEP, many, 0)
        left = seen % STEP
        done = seen - left
        number = STEP // 2
        while number:
            pl.when((left & number) != 0)(
                functools.partial(update, done + (left & ~(2 * number - 1)), number)
            )
            number //= 2

    for group, bound, rows_ref, state in zip(groups, bounds, rows_refs, states):
        if group in fresh:
            state[0][...] = jnp.full_like(state[0], BIG)
            state[1][...] = jnp.zeros_like(state[1])
            state[2][...] = jnp.zeros_like(state[2])
        attend_group(rows_ref, state, jnp.where(bound == high, some, both))

    if pack:
        largest_ref, totals_ref, summed_ref = states[0]
        count = summed_ref.shape[0]
        lane = lax.broadcasted_iota(jnp.int32, (count, HD), 1)
        total = jnp.sum(totals_ref[...], axis=1, keepdims=True)
        packed_refs[0][:count, :] = summed_ref[...]
        packed_refs[0][count:, :] = jnp.where(lane < HD // 2, largest_ref[...], total)


def finish_kernel(heads, largest_ref, totals_ref, summed_ref, packed_ref, out_ref):
    token = out_ref.shape[0]
    count = summed_ref.shape[0]
    for at in range(heads):
        first = (pl.program_id(0) * heads + at) * token
        rows = pl.ds(pl.multiple_of(first, token), token)
        packed = packed_ref[pl.ds(pl.multiple_of(count + first, token), token), :]
        largest = largest_ref[rows, :]
        other = packed[:, :1]
        top = jnp.maximum(largest, other)
        mine, theirs = jnp.exp2((largest - top) * TO_LOG2), jnp.exp2((other - top) * TO_LOG2)
        total = jnp.sum(totals_ref[rows, :], axis=1, keepdims=True) * mine
        total += packed[:, HD // 2 : HD // 2 + 1] * theirs
        summed = summed_ref[rows, :] * mine + packed_ref[rows, :] * theirs
        out_ref[:, at * HD : (at + 1) * HD] = summed / total


def params(rows, token, blocks):
    return dict(
        compiler_params=pltpu.CompilerParams(vmem_limit_bytes=LIMIT),
        cost_estimate=pl.CostEstimate(
            flops=6 * rows * HD * token * blocks,
            transcendentals=rows * token * blocks,
            bytes_accessed=1 << 20,
        ),
    )


def attend_own(queries, own):
    token, width = queries.shape
    rows = width // HD * token
    sums = jax.ShapeDtypeStruct((rows, HD), jnp.float32)
    result = pl.pallas_call(
        own_kernel,
        out_shape=[jax.ShapeDtypeStruct((rows, HD), jnp.bfloat16), sums, sums, sums],
        in_specs=[VMEM] * 2,
        out_specs=[VMEM] * 4,
        **params(rows, token, 1),
    )(queries, own)
    return result[0], tuple(result[1:])


def attend(starts, rows, states, items, groups, size_key, token, pack=False):
    count = rows[0].shape[0]
    arrays, pieces = zip(*items)
    blocks = sum(array.shape[0] for array in arrays) // (2 * token)
    fresh = tuple(group for group in groups if states[group] is None)
    sums = [jax.ShapeDtypeStruct((count, HD), jnp.float32)] * 3
    outs = sums * len(groups)
    if pack:
        outs.append(jax.ShapeDtypeStruct((2 * count, HD), jnp.float32))
    operands = [starts, *(rows[group] for group in groups), *arrays]
    aliases = {}
    for at, group in enumerate(groups):
        if group not in fresh:
            aliases.update({len(operands) + index: 3 * at + index for index in range(3)})
            operands += states[group]
    kernel = functools.partial(attend_kernel, pieces, groups, fresh, pack, size_key, token)
    result = pl.pallas_call(
        kernel,
        out_shape=outs,
        in_specs=[SMEM] + [VMEM] * (len(operands) - 1),
        out_specs=[VMEM] * len(outs),
        input_output_aliases=aliases,
        scratch_shapes=[pltpu.VMEM((blocks * token, HD), jnp.bfloat16)] * 2,
        **params(count * len(groups), token, blocks),
    )(*operands)
    states = list(states)
    for at, group in enumerate(groups):
        states[group] = tuple(result[3 * at : 3 * at + 3])
    return states, result[-1]


def finish(sums, packed, shape):
    token, width = shape
    heads = 2 if width % (2 * HD) == 0 else 1
    return pl.pallas_call(
        functools.partial(finish_kernel, heads),
        grid=(width // (heads * HD),),
        out_shape=jax.ShapeDtypeStruct(shape, jnp.float32),
        in_specs=[VMEM] * 4,
        out_specs=pl.BlockSpec((token, heads * HD), lambda step: (0, step)),
        **params(width // HD * token, token, 1),
    )(*sums, packed)


def move(array, mask_even, mask_odd, place):
    size_query, size_key = lax.axis_size("pb"), lax.axis_size("ka")
    pairs = []
    for query in range(size_query):
        source = query ^ (mask_odd if query % 2 else mask_even)
        for key in range(size_key):
            pairs.append((source * size_key + (key ^ place), query * size_key + key))
    return lax.ppermute(array, AXES, pairs)


def stages(size_query):
    bits = [1 << at for at in range(1, size_query.bit_length() - 1)]
    return [bits[at : at + 2] for at in range(0, len(bits), 2)]


def paired(size_query, size_key):
    plan = stages(size_query)
    return len(plan) == 1 and len(plan[0]) == 2 and size_key > 1


def spread(item, bits):
    array, parts = item
    one, two = bits[0], bits[-1]
    near = (move(array, one, two, 0), shifted(parts, one, two))
    if one == two:
        return near, None, None
    side = (move(array, two, one, 0), shifted(parts, two, one))
    far = (move(near[0], two, one, 0), shifted(near[1], two, one))
    return near, side, far


def shifted(parts, even, odd):
    return tuple((at, number, base, one ^ even, two ^ odd) for at, number, base, one, two in parts)


def joined(first, second):
    (one, parts), (two, more) = first, second
    skip = sum(number for _, number, *_ in parts)
    more = tuple((at + skip, *rest) for at, *rest in more)
    return jnp.concatenate([one, two], axis=0), parts + more


def gathered_attention(queries, keys, values, positions):
    token = queries.shape[0]
    size_query, size_key = lax.axis_size("pb"), lax.axis_size("ka")
    assert size_query & (size_query - 1) == 0 and size_key & (size_key - 1) == 0 and size_query > 1
    starts = positions.reshape(-1, token)[:, 0]
    own = jnp.concatenate([keys, values], axis=0)
    column = [own] + [move(own, 0, 0, place) for place in range(1, size_key)]
    half = max(size_key // 2, 1)
    held = [
        (jnp.concatenate(column[base : base + half], axis=0), ((0, half, base, 0, 0),))
        for base in range(0, size_key, half)
    ]

    rows, sums = attend_own(queries, own)
    rows = (rows, move(rows, 1, 1, 0))
    plan = stages(size_query)
    if paired(size_query, size_key):
        (lower, upper), (one, two) = held, plan[0]
        array, parts = lower
        near = (move(array, one, two, 0), shifted(parts, one, two))
        side = (move(array, two, one, 0), shifted(parts, two, one))
        array, parts = upper
        near_up = (move(array, one, two, 0), shifted(parts, one, two))
        array, parts = joined(near, upper)
        mixed = (move(array, two, one, 0), shifted(parts, two, one))
        array, parts = near_up
        far_up = (move(array, two, one, 0), shifted(parts, two, one))
        early = [[lower], [near, side]]
        late = [[upper, near_up, mixed], [far_up]]
    else:
        early = [held]
        for bits in plan:
            more = [item for piece in held for item in spread(piece, bits) if item is not None]
            early.append(more)
            held = held + more
        early, late = early[:-1], early[-1:]

    states = [sums, None]
    attend_to = functools.partial(attend, size_key=size_key, token=token)
    number = 0
    steps = [(group, (0, 1)) for group in early] + [(group, (1,)) for group in late]
    for number, (group, who) in enumerate(steps):
        pack = number == len(steps) - 1
        states, packed = attend_to(starts, rows, states, group, who, pack=pack)
    packed = move(packed, 1, 1, 0)
    rest = [item for group in late for item in group]
    states, _ = attend_to(starts, rows, states, rest, (0,))
    return finish(states[0], packed, queries.shape)


def solution(mesh):
    return jax.shard_map(
        gathered_attention,
        mesh=mesh,
        in_specs=(P(AXES, None), P(AXES, None), P(AXES, None), P()),
        out_specs=P(AXES, None),
        check_vma=False,
    )
```

```python
import functools
import math

import jax
import jax.numpy as jnp
from jax import lax
from jax.experimental import pallas as pl
from jax.experimental.pallas import tpu as pltpu
from jax.sharding import PartitionSpec as P


HD = 128
AXES = ("pb", "ka")
BIG = -1e30
STEP = 4
LIMIT = 24 << 20

VMEM = pl.BlockSpec(memory_space=pltpu.VMEM)
SMEM = pl.BlockSpec(memory_space=pltpu.SMEM)


def combine(rows, keys, values, sums, to_log2, mask=None):
    score = lax.dot_general(
        rows, keys, (((1,), (1,)), ((), ())), preferred_element_type=jnp.float32
    )
    if mask is not None:
        score = jnp.where(mask, score, BIG)
    parts = [score[:, at : at + HD] for at in range(0, keys.shape[0], HD)]
    top = jnp.max(functools.reduce(jnp.maximum, parts), axis=1, keepdims=True)
    if sums is None:
        top = jnp.broadcast_to(top, (rows.shape[0], HD))
    else:
        top = jnp.maximum(sums[0], top)
    weights = [jnp.exp2((part - top) * to_log2) for part in parts]
    if mask is not None:
        weights = [jnp.where(mask, weight, 0.0) for weight in weights]
    total = functools.reduce(jnp.add, weights)
    weight = jnp.concatenate(weights, axis=1) if len(weights) > 1 else weights[0]
    high = weight.astype(jnp.bfloat16)
    low = (weight - high.astype(jnp.float32)).astype(jnp.bfloat16)
    over = (((1,), (0,)), ((), ()))
    result = lax.dot_general(high, values, over, preferred_element_type=jnp.float32)
    result += lax.dot_general(low, values, over, preferred_element_type=jnp.float32)
    if sums is None:
        return top, total, result
    largest, totals, summed = sums
    factor = jnp.exp2((largest - top) * to_log2)
    return top, totals * factor + total, summed * factor + result


TO_LOG2 = math.log2(math.e) / HD**0.5


def own_kernel(
    queries_ref, other_ref, own_ref, rows_ref, other_rows_ref, largest_ref, totals_ref, summed_ref
):
    token, width = queries_ref.shape
    heads = width // HD
    for head in range(heads):
        rows, columns = slice(head * token, (head + 1) * token), slice(head * HD, (head + 1) * HD)
        rows_ref[rows, :] = queries_ref[:, columns]
        other_rows_ref[rows, :] = other_ref[:, columns]
    shape = (heads, token, token)
    causal = lax.broadcasted_iota(jnp.int32, shape, 2) <= lax.broadcasted_iota(jnp.int32, shape, 1)
    keys, values = own_ref[:token, :], own_ref[token:, :]
    mask = causal.reshape(heads * token, token)
    new = combine(rows_ref[...], keys, values, None, TO_LOG2, mask)
    for held, value in zip((largest_ref, totals_ref, summed_ref), new):
        held[...] = value


def attend_kernel(pieces, groups, fresh, pack, size_key, token, *refs):
    refs = list(refs)
    take = lambda number: [refs.pop(0) for _ in range(number)]
    (starts_ref,) = take(1)
    rows_refs = take(len(groups))
    block_refs = take(len(pieces))
    take(3 * (len(groups) - len(fresh)))
    states = [take(3) for _ in groups]
    packed_refs = take(1 if pack else 0)
    keys_ref, values_ref = take(2)

    own_pb, own_ka = lax.axis_index("pb"), lax.axis_index("ka")
    core = own_pb % 2
    bounds = [starts_ref[(own_pb ^ group) * size_key + own_ka] for group in groups]
    low = functools.reduce(jnp.minimum, bounds)
    high = functools.reduce(jnp.maximum, bounds)

    def compact(seen, inside):
        for ref, parts in zip(block_refs, pieces):
            for offset, number, base, mask_even, mask_odd in parts:
                source = (own_pb ^ jnp.where(core == 0, mask_even, mask_odd)) * size_key
                for at in range(number):
                    visible = inside(starts_ref[source + (own_ka ^ (base + at))])
                    row = (offset + at) * 2 * token

                    @pl.when(visible)
                    def _():
                        target = pl.ds(pl.multiple_of(seen * token, token), token)
                        keys_ref[target, :] = ref[row : row + token, :]
                        values_ref[target, :] = ref[row + token : row + 2 * token, :]

                    seen = seen + visible.astype(jnp.int32)
        return seen

    both = compact(jnp.int32(0), lambda start: start < low)
    some = both
    if len(groups) > 1:
        some = compact(both, lambda start: (start >= low) & (start < high))

    def attend_group(rows_ref, state, seen):
        def update(first, number):
            part = pl.ds(pl.multiple_of(first * token, token), number * token)
            sums = [held[...] for held in state]
            new = combine(rows_ref[...], keys_ref[part, :], values_ref[part, :], sums, TO_LOG2)
            for held, value in zip(state, new):
                held[...] = value

        def many(index, _):
            update(index * STEP, STEP)
            return 0

        lax.fori_loop(0, seen // STEP, many, 0)
        left = seen % STEP
        done = seen - left
        number = STEP // 2
        while number:
            pl.when((left & number) != 0)(
                functools.partial(update, done + (left & ~(2 * number - 1)), number)
            )
            number //= 2

    for group, bound, rows_ref, state in zip(groups, bounds, rows_refs, states):
        if group in fresh:
            state[0][...] = jnp.full_like(state[0], BIG)
            state[1][...] = jnp.zeros_like(state[1])
            state[2][...] = jnp.zeros_like(state[2])
        attend_group(rows_ref, state, jnp.where(bound == high, some, both))

    if pack:
        largest_ref, totals_ref, summed_ref = states[0]
        count = summed_ref.shape[0]
        lane = lax.broadcasted_iota(jnp.int32, (count, HD), 1)
        total = jnp.sum(totals_ref[...], axis=1, keepdims=True)
        packed_refs[0][:count, :] = summed_ref[...]
        packed_refs[0][count:, :] = jnp.where(lane < HD // 2, largest_ref[...], total)


def finish_kernel(largest_ref, totals_ref, summed_ref, packed_ref, out_ref):
    token, width = out_ref.shape
    count = summed_ref.shape[0]
    for head in range(width // HD):
        rows = slice(head * token, (head + 1) * token)
        packed = packed_ref[count + head * token : count + (head + 1) * token, :]
        largest = largest_ref[rows, :]
        other = packed[:, :1]
        top = jnp.maximum(largest, other)
        mine, theirs = jnp.exp2((largest - top) * TO_LOG2), jnp.exp2((other - top) * TO_LOG2)
        total = jnp.sum(totals_ref[rows, :], axis=1, keepdims=True) * mine
        total += packed[:, HD // 2 : HD // 2 + 1] * theirs
        summed = summed_ref[rows, :] * mine + packed_ref[rows, :] * theirs
        out_ref[:, head * HD : (head + 1) * HD] = summed / total


def params(rows, token, blocks):
    return dict(
        compiler_params=pltpu.CompilerParams(vmem_limit_bytes=LIMIT),
        cost_estimate=pl.CostEstimate(
            flops=6 * rows * HD * token * blocks,
            transcendentals=rows * token * blocks,
            bytes_accessed=1 << 20,
        ),
    )


def attend_own(queries, other, own):
    token, width = queries.shape
    count = width // HD * token
    rows = jax.ShapeDtypeStruct((count, HD), jnp.bfloat16)
    sums = jax.ShapeDtypeStruct((count, HD), jnp.float32)
    result = pl.pallas_call(
        own_kernel,
        out_shape=[rows, rows, sums, sums, sums],
        in_specs=[VMEM] * 3,
        out_specs=[VMEM] * 5,
        **params(count, token, 1),
    )(queries, other, own)
    return tuple(result[:2]), tuple(result[2:])


def attend(starts, rows, states, items, groups, size_key, token, pack=False):
    count = rows[0].shape[0]
    arrays, pieces = zip(*items)
    blocks = sum(array.shape[0] for array in arrays) // (2 * token)
    fresh = tuple(group for group in groups if states[group] is None)
    sums = [jax.ShapeDtypeStruct((count, HD), jnp.float32)] * 3
    outs = sums * len(groups)
    if pack:
        outs.append(jax.ShapeDtypeStruct((2 * count, HD), jnp.float32))
    operands = [starts, *(rows[group] for group in groups), *arrays]
    aliases = {}
    for at, group in enumerate(groups):
        if group not in fresh:
            aliases.update({len(operands) + index: 3 * at + index for index in range(3)})
            operands += states[group]
    kernel = functools.partial(attend_kernel, pieces, groups, fresh, pack, size_key, token)
    result = pl.pallas_call(
        kernel,
        out_shape=outs,
        in_specs=[SMEM] + [VMEM] * (len(operands) - 1),
        out_specs=[VMEM] * len(outs),
        input_output_aliases=aliases,
        scratch_shapes=[pltpu.VMEM((blocks * token, HD), jnp.bfloat16)] * 2,
        **params(count * len(groups), token, blocks),
    )(*operands)
    states = list(states)
    for at, group in enumerate(groups):
        states[group] = tuple(result[3 * at : 3 * at + 3])
    return states, result[-1]


def finish(sums, packed, shape):
    token, width = shape
    return pl.pallas_call(
        finish_kernel,
        out_shape=jax.ShapeDtypeStruct(shape, jnp.float32),
        in_specs=[VMEM] * 4,
        out_specs=VMEM,
        **params(width // HD * token, token, 1),
    )(*sums, packed)


def move(array, mask_even, mask_odd, place):
    size_query, size_key = lax.axis_size("pb"), lax.axis_size("ka")
    pairs = []
    for query in range(size_query):
        source = query ^ (mask_odd if query % 2 else mask_even)
        for key in range(size_key):
            pairs.append((source * size_key + (key ^ place), query * size_key + key))
    return lax.ppermute(array, AXES, pairs)


def stages(size_query):
    bits = [1 << at for at in range(1, size_query.bit_length() - 1)]
    return [bits[at : at + 2] for at in range(0, len(bits), 2)]


def paired(size_query, size_key):
    plan = stages(size_query)
    return len(plan) == 1 and len(plan[0]) == 2 and size_key > 1


def spread(item, bits):
    array, parts = item
    one, two = bits[0], bits[-1]
    near = (move(array, one, two, 0), shifted(parts, one, two))
    if one == two:
        return near, None, None
    side = (move(array, two, one, 0), shifted(parts, two, one))
    far = (move(near[0], two, one, 0), shifted(near[1], two, one))
    return near, side, far


def shifted(parts, even, odd):
    return tuple((at, number, base, one ^ even, two ^ odd) for at, number, base, one, two in parts)


def joined(first, second):
    (one, parts), (two, more) = first, second
    skip = sum(number for _, number, *_ in parts)
    more = tuple((at + skip, *rest) for at, *rest in more)
    return jnp.concatenate([one, two], axis=0), parts + more


def gathered_attention(queries, keys, values, positions):
    token = queries.shape[0]
    size_query, size_key = lax.axis_size("pb"), lax.axis_size("ka")
    assert size_query & (size_query - 1) == 0 and size_key & (size_key - 1) == 0 and size_query > 1
    starts = positions.reshape(-1, token)[:, 0]
    own = jnp.concatenate([keys, values], axis=0)
    other = move(queries, 1, 1, 0)
    column = [own] + [move(own, 0, 0, place) for place in range(1, size_key)]
    half = max(size_key // 2, 1)
    held = [
        (jnp.concatenate(column[base : base + half], axis=0), ((0, half, base, 0, 0),))
        for base in range(0, size_key, half)
    ]

    rows, sums = attend_own(queries, other, own)
    plan = stages(size_query)
    if paired(size_query, size_key):
        (lower, upper), (one, two) = held, plan[0]
        array, parts = lower
        near = (move(array, one, two, 0), shifted(parts, one, two))
        side = (move(array, two, one, 0), shifted(parts, two, one))
        array, parts = upper
        near_up = (move(array, one, two, 0), shifted(parts, one, two))
        array, parts = joined(near, upper)
        mixed = (move(array, two, one, 0), shifted(parts, two, one))
        array, parts = near_up
        far_up = (move(array, two, one, 0), shifted(parts, two, one))
        early = [[lower, near, side]]
        late = [[upper, near_up, mixed], [far_up]]
    else:
        early = [held]
        for bits in plan:
            more = [item for piece in held for item in spread(piece, bits) if item is not None]
            early.append(more)
            held = held + more
        early, late = early[:-1], early[-1:]

    states = [sums, None]
    attend_to = functools.partial(attend, size_key=size_key, token=token)
    number = 0
    steps = [(group, (0, 1)) for group in early] + [(group, (1,)) for group in late]
    for number, (group, who) in enumerate(steps):
        pack = number == len(steps) - 1
        states, packed = attend_to(starts, rows, states, group, who, pack=pack)
    packed = move(packed, 1, 1, 0)
    rest = [item for group in late for item in group]
    states, _ = attend_to(starts, rows, states, rest, (0,))
    return finish(states[0], packed, queries.shape)


def solution(mesh):
    return jax.shard_map(
        gathered_attention,
        mesh=mesh,
        in_specs=(P(AXES, None), P(AXES, None), P(AXES, None), P()),
        out_specs=P(AXES, None),
        check_vma=False,
    )
```

```python
import functools
import math

import jax
import jax.numpy as jnp
from jax import lax
from jax.experimental import pallas as pl
from jax.experimental.pallas import tpu as pltpu
from jax.sharding import PartitionSpec as P


HD = 128
AXES = ("pb", "ka")
BIG = -1e30
STEP = 4
LIMIT = 24 << 20

VMEM = pl.BlockSpec(memory_space=pltpu.VMEM)
SMEM = pl.BlockSpec(memory_space=pltpu.SMEM)


def combine(rows, keys, values, sums, to_log2, mask=None):
    score = lax.dot_general(
        rows, keys, (((1,), (1,)), ((), ())), preferred_element_type=jnp.float32
    )
    if mask is not None:
        score = jnp.where(mask, score, BIG)
    parts = [score[:, at : at + HD] for at in range(0, keys.shape[0], HD)]
    top = jnp.max(functools.reduce(jnp.maximum, parts), axis=1, keepdims=True)
    if sums is None:
        top = jnp.broadcast_to(top, (rows.shape[0], HD))
    else:
        top = jnp.maximum(sums[0], top)
    weights = [jnp.exp2((part - top) * to_log2) for part in parts]
    if mask is not None:
        weights = [jnp.where(mask, weight, 0.0) for weight in weights]
    total = functools.reduce(jnp.add, weights)
    weight = jnp.concatenate(weights, axis=1) if len(weights) > 1 else weights[0]
    high = weight.astype(jnp.bfloat16)
    low = (weight - high.astype(jnp.float32)).astype(jnp.bfloat16)
    over = (((1,), (0,)), ((), ()))
    result = lax.dot_general(high, values, over, preferred_element_type=jnp.float32)
    result += lax.dot_general(low, values, over, preferred_element_type=jnp.float32)
    if sums is None:
        return top, total, result
    largest, totals, summed = sums
    factor = jnp.exp2((largest - top) * to_log2)
    return top, totals * factor + total, summed * factor + result


TO_LOG2 = math.log2(math.e) / HD**0.5


def pack_kernel(keys_ref, values_ref, out_ref, done):
    token = keys_ref.shape[0]
    copies = [
        pltpu.make_async_copy(keys_ref, out_ref.at[:token, :], done.at[0]),
        pltpu.make_async_copy(values_ref, out_ref.at[token:, :], done.at[1]),
    ]
    for copy in copies:
        copy.start()
    for copy in copies:
        copy.wait()


def own_kernel(
    queries_ref, other_ref, own_ref, rows_ref, other_rows_ref, largest_ref, totals_ref, summed_ref
):
    token, width = queries_ref.shape
    heads = width // HD
    for head in range(heads):
        rows, columns = slice(head * token, (head + 1) * token), slice(head * HD, (head + 1) * HD)
        rows_ref[rows, :] = queries_ref[:, columns]
        other_rows_ref[rows, :] = other_ref[:, columns]
    shape = (heads, token, token)
    causal = lax.broadcasted_iota(jnp.int32, shape, 2) <= lax.broadcasted_iota(jnp.int32, shape, 1)
    keys, values = own_ref[:token, :], own_ref[token:, :]
    mask = causal.reshape(heads * token, token)
    new = combine(rows_ref[...], keys, values, None, TO_LOG2, mask)
    for held, value in zip((largest_ref, totals_ref, summed_ref), new):
        held[...] = value


def attend_kernel(pieces, groups, fresh, pack, size_key, token, *refs):
    refs = list(refs)
    take = lambda number: [refs.pop(0) for _ in range(number)]
    (starts_ref,) = take(1)
    rows_refs = take(len(groups))
    block_refs = take(len(pieces))
    take(3 * (len(groups) - len(fresh)))
    states = [take(3) for _ in groups]
    packed_refs = take(1 if pack else 0)
    keys_ref, values_ref = take(2)

    own_pb, own_ka = lax.axis_index("pb"), lax.axis_index("ka")
    core = own_pb % 2
    bounds = [starts_ref[(own_pb ^ group) * size_key + own_ka] for group in groups]
    low = functools.reduce(jnp.minimum, bounds)
    high = functools.reduce(jnp.maximum, bounds)

    def compact(seen, inside):
        for ref, parts in zip(block_refs, pieces):
            for offset, number, base, mask_even, mask_odd in parts:
                source = (own_pb ^ jnp.where(core == 0, mask_even, mask_odd)) * size_key
                for at in range(number):
                    visible = inside(starts_ref[source + (own_ka ^ (base + at))])
                    row = (offset + at) * 2 * token

                    @pl.when(visible)
                    def _():
                        target = pl.ds(pl.multiple_of(seen * token, token), token)
                        keys_ref[target, :] = ref[row : row + token, :]
                        values_ref[target, :] = ref[row + token : row + 2 * token, :]

                    seen = seen + visible.astype(jnp.int32)
        return seen

    both = compact(jnp.int32(0), lambda start: start < low)
    some = both
    if len(groups) > 1:
        some = compact(both, lambda start: (start >= low) & (start < high))

    def attend_group(rows_ref, state, seen):
        def update(first, number):
            part = pl.ds(pl.multiple_of(first * token, token), number * token)
            sums = [held[...] for held in state]
            new = combine(rows_ref[...], keys_ref[part, :], values_ref[part, :], sums, TO_LOG2)
            for held, value in zip(state, new):
                held[...] = value

        def many(index, _):
            update(index * STEP, STEP)
            return 0

        lax.fori_loop(0, seen // STEP, many, 0)
        left = seen % STEP
        done = seen - left
        number = STEP // 2
        while number:
            pl.when((left & number) != 0)(
                functools.partial(update, done + (left & ~(2 * number - 1)), number)
            )
            number //= 2

    for group, bound, rows_ref, state in zip(groups, bounds, rows_refs, states):
        if group in fresh:
            state[0][...] = jnp.full_like(state[0], BIG)
            state[1][...] = jnp.zeros_like(state[1])
            state[2][...] = jnp.zeros_like(state[2])
        attend_group(rows_ref, state, jnp.where(bound == high, some, both))

    if pack:
        largest_ref, totals_ref, summed_ref = states[0]
        count = summed_ref.shape[0]
        lane = lax.broadcasted_iota(jnp.int32, (count, HD), 1)
        total = jnp.sum(totals_ref[...], axis=1, keepdims=True)
        packed_refs[0][:count, :] = summed_ref[...]
        packed_refs[0][count:, :] = jnp.where(lane < HD // 2, largest_ref[...], total)


def finish_kernel(largest_ref, totals_ref, summed_ref, packed_ref, out_ref):
    token, width = out_ref.shape
    count = summed_ref.shape[0]
    for head in range(width // HD):
        rows = slice(head * token, (head + 1) * token)
        packed = packed_ref[count + head * token : count + (head + 1) * token, :]
        largest = largest_ref[rows, :]
        other = packed[:, :1]
        top = jnp.maximum(largest, other)
        mine, theirs = jnp.exp2((largest - top) * TO_LOG2), jnp.exp2((other - top) * TO_LOG2)
        total = jnp.sum(totals_ref[rows, :], axis=1, keepdims=True) * mine
        total += packed[:, HD // 2 : HD // 2 + 1] * theirs
        summed = summed_ref[rows, :] * mine + packed_ref[rows, :] * theirs
        out_ref[:, head * HD : (head + 1) * HD] = summed / total


def params(rows, token, blocks):
    return dict(
        compiler_params=pltpu.CompilerParams(vmem_limit_bytes=LIMIT),
        cost_estimate=pl.CostEstimate(
            flops=6 * rows * HD * token * blocks,
            transcendentals=rows * token * blocks,
            bytes_accessed=1 << 20,
        ),
    )


def packed_blocks(keys, values):
    token, width = keys.shape
    return pl.pallas_call(
        pack_kernel,
        out_shape=jax.ShapeDtypeStruct((2 * token, width), keys.dtype),
        in_specs=[pl.BlockSpec(memory_space=pltpu.HBM)] * 2,
        out_specs=VMEM,
        scratch_shapes=[pltpu.SemaphoreType.DMA((2,))],
        compiler_params=pltpu.CompilerParams(vmem_limit_bytes=LIMIT),
    )(*(pltpu.with_memory_space_constraint(array, pltpu.HBM) for array in (keys, values)))


def attend_own(queries, other, own):
    token, width = queries.shape
    count = width // HD * token
    rows = jax.ShapeDtypeStruct((count, HD), jnp.bfloat16)
    sums = jax.ShapeDtypeStruct((count, HD), jnp.float32)
    result = pl.pallas_call(
        own_kernel,
        out_shape=[rows, rows, sums, sums, sums],
        in_specs=[VMEM] * 3,
        out_specs=[VMEM] * 5,
        **params(count, token, 1),
    )(queries, other, own)
    return tuple(result[:2]), tuple(result[2:])


def attend(starts, rows, states, items, groups, size_key, token, pack=False):
    count = rows[0].shape[0]
    arrays, pieces = zip(*items)
    blocks = sum(array.shape[0] for array in arrays) // (2 * token)
    fresh = tuple(group for group in groups if states[group] is None)
    sums = [jax.ShapeDtypeStruct((count, HD), jnp.float32)] * 3
    outs = sums * len(groups)
    if pack:
        outs.append(jax.ShapeDtypeStruct((2 * count, HD), jnp.float32))
    operands = [starts, *(rows[group] for group in groups), *arrays]
    aliases = {}
    for at, group in enumerate(groups):
        if group not in fresh:
            aliases.update({len(operands) + index: 3 * at + index for index in range(3)})
            operands += states[group]
    kernel = functools.partial(attend_kernel, pieces, groups, fresh, pack, size_key, token)
    result = pl.pallas_call(
        kernel,
        out_shape=outs,
        in_specs=[SMEM] + [VMEM] * (len(operands) - 1),
        out_specs=[VMEM] * len(outs),
        input_output_aliases=aliases,
        scratch_shapes=[pltpu.VMEM((blocks * token, HD), jnp.bfloat16)] * 2,
        **params(count * len(groups), token, blocks),
    )(*operands)
    states = list(states)
    for at, group in enumerate(groups):
        states[group] = tuple(result[3 * at : 3 * at + 3])
    return states, result[-1]


def finish(sums, packed, shape):
    token, width = shape
    return pl.pallas_call(
        finish_kernel,
        out_shape=jax.ShapeDtypeStruct(shape, jnp.float32),
        in_specs=[VMEM] * 4,
        out_specs=VMEM,
        **params(width // HD * token, token, 1),
    )(*sums, packed)


def move(array, mask_even, mask_odd, place):
    size_query, size_key = lax.axis_size("pb"), lax.axis_size("ka")
    pairs = []
    for query in range(size_query):
        source = query ^ (mask_odd if query % 2 else mask_even)
        for key in range(size_key):
            pairs.append((source * size_key + (key ^ place), query * size_key + key))
    return lax.ppermute(array, AXES, pairs)


def stages(size_query):
    bits = [1 << at for at in range(1, size_query.bit_length() - 1)]
    return [bits[at : at + 2] for at in range(0, len(bits), 2)]


def paired(size_query, size_key):
    plan = stages(size_query)
    return len(plan) == 1 and len(plan[0]) == 2 and size_key > 1


def spread(item, bits):
    array, parts = item
    one, two = bits[0], bits[-1]
    near = (move(array, one, two, 0), shifted(parts, one, two))
    if one == two:
        return near, None, None
    side = (move(array, two, one, 0), shifted(parts, two, one))
    far = (move(near[0], two, one, 0), shifted(near[1], two, one))
    return near, side, far


def shifted(parts, even, odd):
    return tuple((at, number, base, one ^ even, two ^ odd) for at, number, base, one, two in parts)


def gathered_attention(queries, keys, values, positions):
    token = queries.shape[0]
    size_query, size_key = lax.axis_size("pb"), lax.axis_size("ka")
    assert size_query & (size_query - 1) == 0 and size_key & (size_key - 1) == 0 and size_query > 1
    starts = positions.reshape(-1, token)[:, 0]
    own = packed_blocks(keys, values)
    other = move(queries, 1, 1, 0)
    column = [own] + [move(own, 0, 0, place) for place in range(1, size_key)]
    half = max(size_key // 2, 1)
    held = [
        (jnp.concatenate(column[base : base + half], axis=0), ((0, half, base, 0, 0),))
        for base in range(0, size_key, half)
    ]

    rows, sums = attend_own(queries, other, own)
    plan = stages(size_query)
    if paired(size_query, size_key):
        (lower, upper), (one, two) = held, plan[0]
        near, side, far = spread(lower, (one, two))
        near_up, side_up, far_up = spread(upper, (one, two))
        early = [[lower], [near, side], [far, upper]]
        late = [[near_up, side_up, far_up]]
    else:
        early = [held]
        for bits in plan:
            more = [item for piece in held for item in spread(piece, bits) if item is not None]
            early.append(more)
            held = held + more
        early, late = early[:-1], early[-1:]

    states = [sums, None]
    attend_to = functools.partial(attend, size_key=size_key, token=token)
    number = 0
    steps = [(group, (0, 1)) for group in early] + [(group, (1,)) for group in late]
    for number, (group, who) in enumerate(steps):
        pack = number == len(steps) - 1
        states, packed = attend_to(starts, rows, states, group, who, pack=pack)
    packed = move(packed, 1, 1, 0)
    rest = [item for group in late for item in group]
    states, _ = attend_to(starts, rows, states, rest, (0,))
    return finish(states[0], packed, queries.shape)


def solution(mesh):
    return jax.shard_map(
        gathered_attention,
        mesh=mesh,
        in_specs=(P(AXES, None), P(AXES, None), P(AXES, None), P()),
        out_specs=P(AXES, None),
        check_vma=False,
    )
```

```python
import functools
import math

import jax
import jax.numpy as jnp
from jax import lax
from jax.experimental import pallas as pl
from jax.experimental.pallas import tpu as pltpu
from jax.sharding import PartitionSpec as P


HD = 128
AXES = ("pb", "ka")
BIG = -1e30
STEP = 4
LIMIT = 24 << 20

VMEM = pl.BlockSpec(memory_space=pltpu.VMEM)
SMEM = pl.BlockSpec(memory_space=pltpu.SMEM)


def combine(rows, keys, values, sums, to_log2, mask=None, last_counts=None):
    score = lax.dot_general(
        rows, keys, (((1,), (1,)), ((), ())), preferred_element_type=jnp.float32
    )
    if mask is not None:
        score = jnp.where(mask, score, BIG)
    parts = [score[:, at : at + HD] for at in range(0, keys.shape[0], HD)]
    if last_counts is not None:
        parts[-1] = jnp.where(last_counts, parts[-1], BIG)
    top = jnp.max(functools.reduce(jnp.maximum, parts), axis=1, keepdims=True)
    if sums is None:
        top = jnp.broadcast_to(top, (rows.shape[0], HD))
    else:
        top = jnp.maximum(sums[0], top)
    weights = [jnp.exp2((part - top) * to_log2) for part in parts]
    if mask is not None:
        weights = [jnp.where(mask, weight, 0.0) for weight in weights]
    total = functools.reduce(jnp.add, weights)
    highs = [weight.astype(jnp.bfloat16) for weight in weights]
    lows = [
        (weight - high.astype(jnp.float32)).astype(jnp.bfloat16)
        for weight, high in zip(weights, highs)
    ]
    halves = [jnp.concatenate(half, axis=1) if len(half) > 1 else half[0] for half in (highs, lows)]
    result = lax.dot_general(
        jnp.concatenate(halves, axis=0),
        values,
        (((1,), (0,)), ((), ())),
        preferred_element_type=jnp.float32,
    )
    result = result[: rows.shape[0]] + result[rows.shape[0] :]
    if sums is None:
        return top, total, result
    largest, totals, summed = sums
    factor = jnp.exp2((largest - top) * to_log2)
    return top, totals * factor + total, summed * factor + result


TO_LOG2 = math.log2(math.e) / HD**0.5


def pack_kernel(keys_ref, values_ref, out_ref, done):
    token = keys_ref.shape[0]
    copies = [
        pltpu.make_async_copy(keys_ref, out_ref.at[:token, :], done.at[0]),
        pltpu.make_async_copy(values_ref, out_ref.at[token:, :], done.at[1]),
    ]
    for copy in copies:
        copy.start()
    for copy in copies:
        copy.wait()


def own_kernel(
    queries_ref, other_ref, own_ref, rows_ref, other_rows_ref, largest_ref, totals_ref, summed_ref
):
    token, width = queries_ref.shape
    heads = width // HD
    for head in range(heads):
        rows, columns = slice(head * token, (head + 1) * token), slice(head * HD, (head + 1) * HD)
        rows_ref[rows, :] = queries_ref[:, columns]
        other_rows_ref[rows, :] = other_ref[:, columns]
    shape = (heads, token, token)
    causal = lax.broadcasted_iota(jnp.int32, shape, 2) <= lax.broadcasted_iota(jnp.int32, shape, 1)
    keys, values = own_ref[:token, :], own_ref[token:, :]
    mask = causal.reshape(heads * token, token)
    new = combine(rows_ref[...], keys, values, None, TO_LOG2, mask)
    for held, value in zip((largest_ref, totals_ref, summed_ref), new):
        held[...] = value


def attend_kernel(pieces, groups, fresh, pack, size_key, token, *refs):
    refs = list(refs)
    take = lambda number: [refs.pop(0) for _ in range(number)]
    (starts_ref,) = take(1)
    rows_refs = take(len(groups))
    block_refs = take(len(pieces))
    take(3 * (len(groups) - len(fresh)))
    states = [take(3) for _ in groups]
    packed_refs = take(1 if pack else 0)
    keys_ref, values_ref = take(2)

    own_pb, own_ka = lax.axis_index("pb"), lax.axis_index("ka")
    core = own_pb % 2
    bounds = [starts_ref[(own_pb ^ group) * size_key + own_ka] for group in groups]
    low = functools.reduce(jnp.minimum, bounds)
    high = functools.reduce(jnp.maximum, bounds)

    def compact(seen, inside):
        for ref, parts in zip(block_refs, pieces):
            for offset, number, base, mask_even, mask_odd in parts:
                source = (own_pb ^ jnp.where(core == 0, mask_even, mask_odd)) * size_key
                for at in range(number):
                    visible = inside(starts_ref[source + (own_ka ^ (base + at))])
                    row = (offset + at) * 2 * token

                    @pl.when(visible)
                    def _():
                        target = pl.ds(pl.multiple_of(seen * token, token), token)
                        keys_ref[target, :] = ref[row : row + token, :]
                        values_ref[target, :] = ref[row + token : row + 2 * token, :]

                    seen = seen + visible.astype(jnp.int32)
        return seen

    both = compact(jnp.int32(0), lambda start: start < low)
    some = both
    if len(groups) > 1:
        some = compact(both, lambda start: (start >= low) & (start < high))

    @pl.when(some % STEP == STEP - 1)
    def _():
        target = pl.ds(pl.multiple_of(some * token, token), token)
        keys_ref[target, :] = jnp.zeros((token, HD), keys_ref.dtype)
        values_ref[target, :] = jnp.zeros((token, HD), values_ref.dtype)

    def attend_group(rows_ref, state, seen):
        def update(first, number, last_counts=None):
            part = pl.ds(pl.multiple_of(first * token, token), number * token)
            sums = [held[...] for held in state]
            new = combine(
                rows_ref[...],
                keys_ref[part, :],
                values_ref[part, :],
                sums,
                TO_LOG2,
                last_counts=last_counts,
            )
            for held, value in zip(state, new):
                held[...] = value

        def many(index, _):
            first = index * STEP
            update(first, STEP, first + STEP <= seen)
            return 0

        left = seen % STEP
        full = (seen + 1) // STEP
        lax.fori_loop(0, full, many, 0)
        done = full * STEP
        pl.when(left == 1)(functools.partial(update, done, 1))
        pl.when(left == 2)(functools.partial(update, done, 2))

    for group, bound, rows_ref, state in zip(groups, bounds, rows_refs, states):
        if group in fresh:
            state[0][...] = jnp.full_like(state[0], BIG)
            state[1][...] = jnp.zeros_like(state[1])
            state[2][...] = jnp.zeros_like(state[2])
        attend_group(rows_ref, state, jnp.where(bound == high, some, both))

    if pack:
        largest_ref, totals_ref, summed_ref = states[0]
        count = summed_ref.shape[0]
        lane = lax.broadcasted_iota(jnp.int32, (count, HD), 1)
        total = jnp.sum(totals_ref[...], axis=1, keepdims=True)
        packed_refs[0][:count, :] = summed_ref[...]
        packed_refs[0][count:, :] = jnp.where(lane < HD // 2, largest_ref[...], total)


def finish_kernel(largest_ref, totals_ref, summed_ref, packed_ref, out_ref):
    token, width = out_ref.shape
    count = summed_ref.shape[0]
    for head in range(width // HD):
        rows = slice(head * token, (head + 1) * token)
        packed = packed_ref[count + head * token : count + (head + 1) * token, :]
        largest = largest_ref[rows, :]
        other = packed[:, :1]
        top = jnp.maximum(largest, other)
        mine, theirs = jnp.exp2((largest - top) * TO_LOG2), jnp.exp2((other - top) * TO_LOG2)
        total = jnp.sum(totals_ref[rows, :], axis=1, keepdims=True) * mine
        total += packed[:, HD // 2 : HD // 2 + 1] * theirs
        summed = summed_ref[rows, :] * mine + packed_ref[rows, :] * theirs
        out_ref[:, head * HD : (head + 1) * HD] = summed / total


def params(rows, token, blocks):
    return dict(
        compiler_params=pltpu.CompilerParams(vmem_limit_bytes=LIMIT),
        cost_estimate=pl.CostEstimate(
            flops=6 * rows * HD * token * blocks,
            transcendentals=rows * token * blocks,
            bytes_accessed=1 << 20,
        ),
    )


def packed_blocks(keys, values):
    token, width = keys.shape
    return pl.pallas_call(
        pack_kernel,
        out_shape=jax.ShapeDtypeStruct((2 * token, width), keys.dtype),
        in_specs=[pl.BlockSpec(memory_space=pltpu.HBM)] * 2,
        out_specs=VMEM,
        scratch_shapes=[pltpu.SemaphoreType.DMA((2,))],
        compiler_params=pltpu.CompilerParams(vmem_limit_bytes=LIMIT),
    )(*(pltpu.with_memory_space_constraint(array, pltpu.HBM) for array in (keys, values)))


def attend_own(queries, other, own):
    token, width = queries.shape
    count = width // HD * token
    rows = jax.ShapeDtypeStruct((count, HD), jnp.bfloat16)
    sums = jax.ShapeDtypeStruct((count, HD), jnp.float32)
    result = pl.pallas_call(
        own_kernel,
        out_shape=[rows, rows, sums, sums, sums],
        in_specs=[VMEM] * 3,
        out_specs=[VMEM] * 5,
        **params(count, token, 1),
    )(queries, other, own)
    return tuple(result[:2]), tuple(result[2:])


def attend(starts, rows, states, items, groups, size_key, token, pack=False):
    count = rows[0].shape[0]
    arrays, pieces = zip(*items)
    blocks = sum(array.shape[0] for array in arrays) // (2 * token)
    room = -(-blocks // STEP) * STEP * token
    fresh = tuple(group for group in groups if states[group] is None)
    sums = [jax.ShapeDtypeStruct((count, HD), jnp.float32)] * 3
    outs = sums * len(groups)
    if pack:
        outs.append(jax.ShapeDtypeStruct((2 * count, HD), jnp.float32))
    operands = [starts, *(rows[group] for group in groups), *arrays]
    aliases = {}
    for at, group in enumerate(groups):
        if group not in fresh:
            aliases.update({len(operands) + index: 3 * at + index for index in range(3)})
            operands += states[group]
    kernel = functools.partial(attend_kernel, pieces, groups, fresh, pack, size_key, token)
    result = pl.pallas_call(
        kernel,
        out_shape=outs,
        in_specs=[SMEM] + [VMEM] * (len(operands) - 1),
        out_specs=[VMEM] * len(outs),
        input_output_aliases=aliases,
        scratch_shapes=[pltpu.VMEM((room, HD), jnp.bfloat16)] * 2,
        **params(count * len(groups), token, blocks),
    )(*operands)
    states = list(states)
    for at, group in enumerate(groups):
        states[group] = tuple(result[3 * at : 3 * at + 3])
    return states, result[-1]


def finish(sums, packed, shape):
    token, width = shape
    return pl.pallas_call(
        finish_kernel,
        out_shape=jax.ShapeDtypeStruct(shape, jnp.float32),
        in_specs=[VMEM] * 4,
        out_specs=VMEM,
        **params(width // HD * token, token, 1),
    )(*sums, packed)


def move(array, mask_even, mask_odd, place):
    size_query, size_key = lax.axis_size("pb"), lax.axis_size("ka")
    pairs = []
    for query in range(size_query):
        source = query ^ (mask_odd if query % 2 else mask_even)
        for key in range(size_key):
            pairs.append((source * size_key + (key ^ place), query * size_key + key))
    return lax.ppermute(array, AXES, pairs)


def stages(size_query):
    bits = [1 << at for at in range(1, size_query.bit_length() - 1)]
    return [bits[at : at + 2] for at in range(0, len(bits), 2)]


def paired(size_query, size_key):
    plan = stages(size_query)
    return len(plan) == 1 and len(plan[0]) == 2 and size_key > 1


def spread(item, bits):
    array, parts = item
    one, two = bits[0], bits[-1]
    near = (move(array, one, two, 0), shifted(parts, one, two))
    if one == two:
        return near, None, None
    side = (move(array, two, one, 0), shifted(parts, two, one))
    far = (move(near[0], two, one, 0), shifted(near[1], two, one))
    return near, side, far


def shifted(parts, even, odd):
    return tuple((at, number, base, one ^ even, two ^ odd) for at, number, base, one, two in parts)


def gathered_attention(queries, keys, values, positions):
    token = queries.shape[0]
    size_query, size_key = lax.axis_size("pb"), lax.axis_size("ka")
    assert size_query & (size_query - 1) == 0 and size_key & (size_key - 1) == 0 and size_query > 1
    starts = positions.reshape(-1, token)[:, 0]
    own = packed_blocks(keys, values)
    other = move(queries, 1, 1, 0)
    column = [own] + [move(own, 0, 0, place) for place in range(1, size_key)]
    half = max(size_key // 2, 1)
    held = [
        (jnp.concatenate(column[base : base + half], axis=0), ((0, half, base, 0, 0),))
        for base in range(0, size_key, half)
    ]

    rows, sums = attend_own(queries, other, own)
    plan = stages(size_query)
    if paired(size_query, size_key):
        (lower, upper), (one, two) = held, plan[0]
        near, side, far = spread(lower, (one, two))
        near_up, side_up, far_up = spread(upper, (one, two))
        early = [[lower], [near, side], [far, upper, near_up]]
        late = [[side_up, far_up]]
    else:
        early = [held]
        for bits in plan:
            more = [item for piece in held for item in spread(piece, bits) if item is not None]
            early.append(more)
            held = held + more
        early, late = early[:-1], early[-1:]

    states = [sums, None]
    attend_to = functools.partial(attend, size_key=size_key, token=token)
    number = 0
    steps = [(group, (0, 1)) for group in early] + [(group, (1,)) for group in late]
    for number, (group, who) in enumerate(steps):
        pack = number == len(steps) - 1
        states, packed = attend_to(starts, rows, states, group, who, pack=pack)
    packed = move(packed, 1, 1, 0)
    rest = [item for group in late for item in group]
    states, _ = attend_to(starts, rows, states, rest, (0,))
    return finish(states[0], packed, queries.shape)


def solution(mesh):
    return jax.shard_map(
        gathered_attention,
        mesh=mesh,
        in_specs=(P(AXES, None), P(AXES, None), P(AXES, None), P()),
        out_specs=P(AXES, None),
        check_vma=False,
    )
```

```python
import functools
import math

import jax
import jax.numpy as jnp
from jax import lax
from jax.experimental import pallas as pl
from jax.experimental.pallas import tpu as pltpu
from jax.sharding import PartitionSpec as P


HD = 128
AXES = ("pb", "ka")
BIG = -1e30
STEP = 4
LIMIT = 24 << 20

VMEM = pl.BlockSpec(memory_space=pltpu.VMEM)
SMEM = pl.BlockSpec(memory_space=pltpu.SMEM)


def combine(rows, keys, values, sums, to_log2, mask=None, last_counts=None):
    score = lax.dot_general(
        rows, keys, (((1,), (1,)), ((), ())), preferred_element_type=jnp.float32
    )
    if mask is not None:
        score = jnp.where(mask, score, BIG)
    parts = [score[:, at : at + HD] for at in range(0, keys.shape[0], HD)]
    if last_counts is not None:
        parts[-1] = jnp.where(last_counts, parts[-1], BIG)
    top = jnp.max(functools.reduce(jnp.maximum, parts), axis=1, keepdims=True)
    if sums is None:
        top = jnp.broadcast_to(top, (rows.shape[0], HD))
    else:
        top = jnp.maximum(sums[0], top)
    weights = [jnp.exp2((part - top) * to_log2) for part in parts]
    if mask is not None:
        weights = [jnp.where(mask, weight, 0.0) for weight in weights]
    total = functools.reduce(jnp.add, weights)
    highs = [weight.astype(jnp.bfloat16) for weight in weights]
    lows = [
        (weight - high.astype(jnp.float32)).astype(jnp.bfloat16)
        for weight, high in zip(weights, highs)
    ]
    halves = [jnp.concatenate(half, axis=1) if len(half) > 1 else half[0] for half in (highs, lows)]
    over = (((1,), (0,)), ((), ()))
    if len(parts) < STEP:
        result = sum(
            lax.dot_general(half, values, over, preferred_element_type=jnp.float32)
            for half in halves
        )
    else:
        both = jnp.concatenate(halves, axis=0)
        result = lax.dot_general(both, values, over, preferred_element_type=jnp.float32)
        result = result[: rows.shape[0]] + result[rows.shape[0] :]
    if sums is None:
        return top, total, result
    largest, totals, summed = sums
    factor = jnp.exp2((largest - top) * to_log2)
    return top, totals * factor + total, summed * factor + result


TO_LOG2 = math.log2(math.e) / HD**0.5


def pack_kernel(keys_ref, values_ref, out_ref, done):
    token = keys_ref.shape[0]
    copies = [
        pltpu.make_async_copy(keys_ref, out_ref.at[:token, :], done.at[0]),
        pltpu.make_async_copy(values_ref, out_ref.at[token:, :], done.at[1]),
    ]
    for copy in copies:
        copy.start()
    for copy in copies:
        copy.wait()


def own_kernel(
    queries_ref, other_ref, own_ref, rows_ref, other_rows_ref, largest_ref, totals_ref, summed_ref
):
    token, width = queries_ref.shape
    heads = width // HD
    for head in range(heads):
        rows, columns = slice(head * token, (head + 1) * token), slice(head * HD, (head + 1) * HD)
        rows_ref[rows, :] = queries_ref[:, columns]
        other_rows_ref[rows, :] = other_ref[:, columns]
    shape = (heads, token, token)
    causal = lax.broadcasted_iota(jnp.int32, shape, 2) <= lax.broadcasted_iota(jnp.int32, shape, 1)
    keys, values = own_ref[:token, :], own_ref[token:, :]
    mask = causal.reshape(heads * token, token)
    new = combine(rows_ref[...], keys, values, None, TO_LOG2, mask)
    for held, value in zip((largest_ref, totals_ref, summed_ref), new):
        held[...] = value


def attend_kernel(pieces, groups, fresh, pack, size_key, token, *refs):
    refs = list(refs)
    take = lambda number: [refs.pop(0) for _ in range(number)]
    (starts_ref,) = take(1)
    rows_refs = take(len(groups))
    block_refs = take(len(pieces))
    take(3 * (len(groups) - len(fresh)))
    states = [take(3) for _ in groups]
    packed_refs = take(1 if pack else 0)
    keys_ref, values_ref = take(2)

    own_pb, own_ka = lax.axis_index("pb"), lax.axis_index("ka")
    core = own_pb % 2

    def compact(bound, places):
        seen = jnp.int32(0)
        for place in places:
            ref = block_refs[place]
            for offset, number, base, mask_even, mask_odd in pieces[place]:
                source = (own_pb ^ jnp.where(core == 0, mask_even, mask_odd)) * size_key
                for at in range(number):
                    visible = starts_ref[source + (own_ka ^ (base + at))] < bound
                    row = (offset + at) * 2 * token

                    @pl.when(visible)
                    def _():
                        target = pl.ds(pl.multiple_of(seen * token, token), token)
                        keys_ref[target, :] = ref[row : row + token, :]
                        values_ref[target, :] = ref[row + token : row + 2 * token, :]

                    seen = seen + visible.astype(jnp.int32)

        @pl.when(seen % STEP == STEP - 1)
        def _():
            target = pl.ds(pl.multiple_of(seen * token, token), token)
            keys_ref[target, :] = jnp.zeros((token, HD), keys_ref.dtype)
            values_ref[target, :] = jnp.zeros((token, HD), values_ref.dtype)

        return seen

    def attend_group(rows_ref, state, seen):
        def update(first, number, last_counts=None):
            part = pl.ds(pl.multiple_of(first * token, token), number * token)
            sums = [held[...] for held in state]
            new = combine(
                rows_ref[...],
                keys_ref[part, :],
                values_ref[part, :],
                sums,
                TO_LOG2,
                last_counts=last_counts,
            )
            for held, value in zip(state, new):
                held[...] = value

        def many(index, _):
            first = index * STEP
            update(first, STEP, first + STEP <= seen)
            return 0

        left = seen % STEP
        full = (seen + 1) // STEP
        lax.fori_loop(0, full, many, 0)
        done = full * STEP
        pl.when(left == 1)(functools.partial(update, done, 1))
        pl.when(left == 2)(functools.partial(update, done, 2))

    for (group, places), rows_ref, state in zip(groups, rows_refs, states):
        if group in fresh:
            state[0][...] = jnp.full_like(state[0], BIG)
            state[1][...] = jnp.zeros_like(state[1])
            state[2][...] = jnp.zeros_like(state[2])
        bound = starts_ref[(own_pb ^ group) * size_key + own_ka]
        attend_group(rows_ref, state, compact(bound, places))

    if pack:
        largest_ref, totals_ref, summed_ref = states[0]
        count = summed_ref.shape[0]
        lane = lax.broadcasted_iota(jnp.int32, (count, HD), 1)
        total = jnp.sum(totals_ref[...], axis=1, keepdims=True)
        packed_refs[0][:count, :] = summed_ref[...]
        packed_refs[0][count:, :] = jnp.where(lane < HD // 2, largest_ref[...], total)


def finish_kernel(largest_ref, totals_ref, summed_ref, packed_ref, out_ref):
    token, width = out_ref.shape
    count = summed_ref.shape[0]
    for head in range(width // HD):
        rows = slice(head * token, (head + 1) * token)
        packed = packed_ref[count + head * token : count + (head + 1) * token, :]
        largest = largest_ref[rows, :]
        other = packed[:, :1]
        top = jnp.maximum(largest, other)
        mine, theirs = jnp.exp2((largest - top) * TO_LOG2), jnp.exp2((other - top) * TO_LOG2)
        total = jnp.sum(totals_ref[rows, :], axis=1, keepdims=True) * mine
        total += packed[:, HD // 2 : HD // 2 + 1] * theirs
        summed = summed_ref[rows, :] * mine + packed_ref[rows, :] * theirs
        out_ref[:, head * HD : (head + 1) * HD] = summed / total


def params(rows, token, blocks):
    return dict(
        compiler_params=pltpu.CompilerParams(vmem_limit_bytes=LIMIT),
        cost_estimate=pl.CostEstimate(
            flops=6 * rows * HD * token * blocks,
            transcendentals=rows * token * blocks,
            bytes_accessed=1 << 20,
        ),
    )


def packed_blocks(keys, values):
    token, width = keys.shape
    return pl.pallas_call(
        pack_kernel,
        out_shape=jax.ShapeDtypeStruct((2 * token, width), keys.dtype),
        in_specs=[pl.BlockSpec(memory_space=pltpu.HBM)] * 2,
        out_specs=VMEM,
        scratch_shapes=[pltpu.SemaphoreType.DMA((2,))],
        compiler_params=pltpu.CompilerParams(vmem_limit_bytes=LIMIT),
    )(*(pltpu.with_memory_space_constraint(array, pltpu.HBM) for array in (keys, values)))


def attend_own(queries, other, own):
    token, width = queries.shape
    count = width // HD * token
    rows = jax.ShapeDtypeStruct((count, HD), jnp.bfloat16)
    sums = jax.ShapeDtypeStruct((count, HD), jnp.float32)
    result = pl.pallas_call(
        own_kernel,
        out_shape=[rows, rows, sums, sums, sums],
        in_specs=[VMEM] * 3,
        out_specs=[VMEM] * 5,
        **params(count, token, 1),
    )(queries, other, own)
    return tuple(result[:2]), tuple(result[2:])


def attend(starts, rows, states, wanted, size_key, token, pack=False):
    count = rows[0].shape[0]
    items = []
    for _, mine in wanted:
        items += [item for item in mine if not any(item is other for other in items)]
    places = [
        (group, tuple(at for item in mine for at, other in enumerate(items) if other is item))
        for group, mine in wanted
    ]
    arrays, pieces = zip(*items)
    blocks = sum(array.shape[0] for array in arrays) // (2 * token)
    room = -(-blocks // STEP) * STEP * token
    fresh = tuple(group for group, _ in wanted if states[group] is None)
    sums = [jax.ShapeDtypeStruct((count, HD), jnp.float32)] * 3
    outs = sums * len(wanted)
    if pack:
        outs.append(jax.ShapeDtypeStruct((2 * count, HD), jnp.float32))
    operands = [starts, *(rows[group] for group, _ in wanted), *arrays]
    aliases = {}
    for at, (group, _) in enumerate(wanted):
        if group not in fresh:
            aliases.update({len(operands) + index: 3 * at + index for index in range(3)})
            operands += states[group]
    kernel = functools.partial(attend_kernel, pieces, places, fresh, pack, size_key, token)
    result = pl.pallas_call(
        kernel,
        out_shape=outs,
        in_specs=[SMEM] + [VMEM] * (len(operands) - 1),
        out_specs=[VMEM] * len(outs),
        input_output_aliases=aliases,
        scratch_shapes=[pltpu.VMEM((room, HD), jnp.bfloat16)] * 2,
        **params(count * len(wanted), token, blocks),
    )(*operands)
    states = list(states)
    for at, (group, _) in enumerate(wanted):
        states[group] = tuple(result[3 * at : 3 * at + 3])
    return states, result[-1]


def finish(sums, packed, shape):
    token, width = shape
    return pl.pallas_call(
        finish_kernel,
        out_shape=jax.ShapeDtypeStruct(shape, jnp.float32),
        in_specs=[VMEM] * 4,
        out_specs=VMEM,
        **params(width // HD * token, token, 1),
    )(*sums, packed)


def move(array, mask_even, mask_odd, place):
    size_query, size_key = lax.axis_size("pb"), lax.axis_size("ka")
    pairs = []
    for query in range(size_query):
        source = query ^ (mask_odd if query % 2 else mask_even)
        for key in range(size_key):
            pairs.append((source * size_key + (key ^ place), query * size_key + key))
    return lax.ppermute(array, AXES, pairs)


def stages(size_query):
    bits = [1 << at for at in range(1, size_query.bit_length() - 1)]
    return [bits[at : at + 2] for at in range(0, len(bits), 2)]


def paired(size_query, size_key):
    plan = stages(size_query)
    return len(plan) == 1 and len(plan[0]) == 2 and size_key > 1


def spread_near(item, bits):
    array, parts = item
    one, two = bits
    near = (move(array, one, two, 0), shifted(parts, one, two))
    side = (move(array, two, one, 0), shifted(parts, two, one))
    return near, side


def spread(item, bits):
    array, parts = item
    one, two = bits[0], bits[-1]
    near = (move(array, one, two, 0), shifted(parts, one, two))
    if one == two:
        return near, None, None
    side = (move(array, two, one, 0), shifted(parts, two, one))
    far = (move(near[0], two, one, 0), shifted(near[1], two, one))
    return near, side, far


def shifted(parts, even, odd):
    return tuple((at, number, base, one ^ even, two ^ odd) for at, number, base, one, two in parts)


def gathered_attention(queries, keys, values, positions):
    token = queries.shape[0]
    size_query, size_key = lax.axis_size("pb"), lax.axis_size("ka")
    assert size_query & (size_query - 1) == 0 and size_key & (size_key - 1) == 0 and size_query > 1
    starts = positions.reshape(-1, token)[:, 0]
    own = packed_blocks(keys, values)
    other = move(queries, 1, 1, 0)
    column = [own] + [move(own, 0, 0, place) for place in range(1, size_key)]
    half = max(size_key // 2, 1)
    held = [
        (jnp.concatenate(column[base : base + half], axis=0), ((0, half, base, 0, 0),))
        for base in range(0, size_key, half)
    ]

    rows, sums = attend_own(queries, other, own)
    plan = stages(size_query)
    if paired(size_query, size_key):
        (lower, upper), (one, two) = held, plan[0]
        near, side = spread_near(lower, (one, two))
        both = one ^ two
        far = (move(lower[0], both, both, 0), shifted(lower[1], both, both))
        near_up, side_up = spread_near(upper, (one, two))
        far_up = (move(upper[0], both, both, 0), shifted(upper[1], both, both))
        steps = [[(0, [lower]), (1, [lower])], [(0, [near, side, far, upper]), (1, [near, side, far, upper])], [(1, [near_up, side_up, far_up])]]
        rest = [near_up, side_up, far_up]
    else:
        shared = [held]
        for bits in plan:
            more = [item for piece in held for item in spread(piece, bits) if item is not None]
            shared.append(more)
            held = held + more
        rest = shared.pop()
        steps = [[(0, group), (1, group)] for group in shared] + [[(1, rest)]]

    states = [sums, None]
    attend_to = functools.partial(attend, size_key=size_key, token=token)
    for number, wanted in enumerate(steps):
        pack = number == len(steps) - 1
        states, packed = attend_to(starts, rows, states, wanted, pack=pack)
    packed = move(packed, 1, 1, 0)
    states, _ = attend_to(starts, rows, states, [(0, rest)])
    return finish(states[0], packed, queries.shape)


def solution(mesh):
    return jax.shard_map(
        gathered_attention,
        mesh=mesh,
        in_specs=(P(AXES, None), P(AXES, None), P(AXES, None), P()),
        out_specs=P(AXES, None),
        check_vma=False,
    )
```

```python
import functools
import math

import jax
import jax.numpy as jnp
from jax import lax
from jax.experimental import pallas as pl
from jax.experimental.pallas import tpu as pltpu
from jax.sharding import PartitionSpec as P


HD = 128
AXES = ("pb", "ka")
BIG = -1e30
STEP = 4
LIMIT = 24 << 20

VMEM = pl.BlockSpec(memory_space=pltpu.VMEM)
SMEM = pl.BlockSpec(memory_space=pltpu.SMEM)


def combine(rows, keys, values, sums, to_log2, mask=None, skip_last=False):
    score = lax.dot_general(
        rows, keys, (((1,), (1,)), ((), ())), preferred_element_type=jnp.float32
    )
    if mask is not None:
        score = jnp.where(mask, score, BIG)
    parts = [score[:, at : at + HD] for at in range(0, keys.shape[0], HD)]
    if skip_last:
        parts[-1] = jnp.full_like(parts[-1], BIG)
    top = jnp.max(functools.reduce(jnp.maximum, parts), axis=1, keepdims=True)
    if sums is None:
        top = jnp.broadcast_to(top, (rows.shape[0], HD))
    else:
        top = jnp.maximum(sums[0], top)
    weights = [jnp.exp2((part - top) * to_log2) for part in parts]
    if mask is not None:
        weights = [jnp.where(mask, weight, 0.0) for weight in weights]
    total = functools.reduce(jnp.add, weights)
    highs = [weight.astype(jnp.bfloat16) for weight in weights]
    lows = [
        (weight - high.astype(jnp.float32)).astype(jnp.bfloat16)
        for weight, high in zip(weights, highs)
    ]
    halves = [jnp.concatenate(half, axis=1) if len(half) > 1 else half[0] for half in (highs, lows)]
    over = (((1,), (0,)), ((), ()))
    if len(parts) < STEP:
        result = sum(
            lax.dot_general(half, values, over, preferred_element_type=jnp.float32)
            for half in halves
        )
    else:
        both = jnp.concatenate(halves, axis=0)
        result = lax.dot_general(both, values, over, preferred_element_type=jnp.float32)
        result = result[: rows.shape[0]] + result[rows.shape[0] :]
    if sums is None:
        return top, total, result
    largest, totals, summed = sums
    factor = jnp.exp2((largest - top) * to_log2)
    return top, totals * factor + total, summed * factor + result


TO_LOG2 = math.log2(math.e) / HD**0.5


def pack_kernel(keys_ref, values_ref, out_ref, done):
    token = keys_ref.shape[0]
    copies = [
        pltpu.make_async_copy(keys_ref, out_ref.at[:token, :], done.at[0]),
        pltpu.make_async_copy(values_ref, out_ref.at[token:, :], done.at[1]),
    ]
    for copy in copies:
        copy.start()
    for copy in copies:
        copy.wait()


def own_kernel(
    queries_ref, other_ref, own_ref, rows_ref, other_rows_ref, largest_ref, totals_ref, summed_ref
):
    token, width = queries_ref.shape
    heads = width // HD
    for head in range(heads):
        rows, columns = slice(head * token, (head + 1) * token), slice(head * HD, (head + 1) * HD)
        rows_ref[rows, :] = queries_ref[:, columns]
        other_rows_ref[rows, :] = other_ref[:, columns]
    shape = (heads, token, token)
    causal = lax.broadcasted_iota(jnp.int32, shape, 2) <= lax.broadcasted_iota(jnp.int32, shape, 1)
    keys, values = own_ref[:token, :], own_ref[token:, :]
    mask = causal.reshape(heads * token, token)
    new = combine(rows_ref[...], keys, values, None, TO_LOG2, mask)
    for held, value in zip((largest_ref, totals_ref, summed_ref), new):
        held[...] = value


def attend_kernel(pieces, groups, fresh, pack, size_key, token, *refs):
    refs = list(refs)
    take = lambda number: [refs.pop(0) for _ in range(number)]
    (starts_ref,) = take(1)
    rows_refs = take(len(groups))
    block_refs = take(len(pieces))
    take(3 * (len(groups) - len(fresh)))
    states = [take(3) for _ in groups]
    packed_refs = take(1 if pack else 0)
    keys_ref, values_ref = take(2)

    own_pb, own_ka = lax.axis_index("pb"), lax.axis_index("ka")
    core = own_pb % 2

    def compact(bound, places):
        seen = jnp.int32(0)
        for place in places:
            ref = block_refs[place]
            for offset, number, base, mask_even, mask_odd in pieces[place]:
                source = (own_pb ^ jnp.where(core == 0, mask_even, mask_odd)) * size_key
                for at in range(number):
                    visible = starts_ref[source + (own_ka ^ (base + at))] < bound
                    row = (offset + at) * 2 * token

                    @pl.when(visible)
                    def _():
                        target = pl.ds(pl.multiple_of(seen * token, token), token)
                        keys_ref[target, :] = ref[row : row + token, :]
                        values_ref[target, :] = ref[row + token : row + 2 * token, :]

                    seen = seen + visible.astype(jnp.int32)

        @pl.when(seen % STEP == STEP - 1)
        def _():
            target = pl.ds(pl.multiple_of(seen * token, token), token)
            keys_ref[target, :] = jnp.zeros((token, HD), keys_ref.dtype)
            values_ref[target, :] = jnp.zeros((token, HD), values_ref.dtype)

        return seen

    def attend_group(rows_ref, state, seen):
        def update(first, number, skip_last=False):
            part = pl.ds(pl.multiple_of(first * token, token), number * token)
            sums = [held[...] for held in state]
            new = combine(
                rows_ref[...],
                keys_ref[part, :],
                values_ref[part, :],
                sums,
                TO_LOG2,
                skip_last=skip_last,
            )
            for held, value in zip(state, new):
                held[...] = value

        def many(index, _):
            update(index * STEP, STEP)
            return 0

        full, left = seen // STEP, seen % STEP
        lax.fori_loop(0, full, many, 0)
        done = full * STEP
        pl.when(left == 1)(functools.partial(update, done, 1))
        pl.when(left == 2)(functools.partial(update, done, 2))
        pl.when(left == 3)(functools.partial(update, done, STEP, True))

    for (group, places), rows_ref, state in zip(groups, rows_refs, states):
        if group in fresh:
            state[0][...] = jnp.full_like(state[0], BIG)
            state[1][...] = jnp.zeros_like(state[1])
            state[2][...] = jnp.zeros_like(state[2])
        bound = starts_ref[(own_pb ^ group) * size_key + own_ka]
        attend_group(rows_ref, state, compact(bound, places))

    if pack:
        largest_ref, totals_ref, summed_ref = states[0]
        count = summed_ref.shape[0]
        lane = lax.broadcasted_iota(jnp.int32, (count, HD), 1)
        total = jnp.sum(totals_ref[...], axis=1, keepdims=True)
        packed_refs[0][:count, :] = summed_ref[...]
        packed_refs[0][count:, :] = jnp.where(lane < HD // 2, largest_ref[...], total)


def finish_kernel(largest_ref, totals_ref, summed_ref, packed_ref, out_ref):
    token, width = out_ref.shape
    count = summed_ref.shape[0]
    for head in range(width // HD):
        rows = slice(head * token, (head + 1) * token)
        packed = packed_ref[count + head * token : count + (head + 1) * token, :]
        largest = largest_ref[rows, :]
        other = packed[:, :1]
        top = jnp.maximum(largest, other)
        mine, theirs = jnp.exp2((largest - top) * TO_LOG2), jnp.exp2((other - top) * TO_LOG2)
        total = jnp.sum(totals_ref[rows, :], axis=1, keepdims=True) * mine
        total += packed[:, HD // 2 : HD // 2 + 1] * theirs
        summed = summed_ref[rows, :] * mine + packed_ref[rows, :] * theirs
        out_ref[:, head * HD : (head + 1) * HD] = summed / total


def params(rows, token, blocks):
    return dict(
        compiler_params=pltpu.CompilerParams(vmem_limit_bytes=LIMIT),
        cost_estimate=pl.CostEstimate(
            flops=6 * rows * HD * token * blocks,
            transcendentals=rows * token * blocks,
            bytes_accessed=1 << 20,
        ),
    )


def packed_blocks(keys, values):
    token, width = keys.shape
    return pl.pallas_call(
        pack_kernel,
        out_shape=jax.ShapeDtypeStruct((2 * token, width), keys.dtype),
        in_specs=[pl.BlockSpec(memory_space=pltpu.HBM)] * 2,
        out_specs=VMEM,
        scratch_shapes=[pltpu.SemaphoreType.DMA((2,))],
        compiler_params=pltpu.CompilerParams(vmem_limit_bytes=LIMIT),
    )(*(pltpu.with_memory_space_constraint(array, pltpu.HBM) for array in (keys, values)))


def attend_own(queries, other, own):
    token, width = queries.shape
    count = width // HD * token
    rows = jax.ShapeDtypeStruct((count, HD), jnp.bfloat16)
    sums = jax.ShapeDtypeStruct((count, HD), jnp.float32)
    result = pl.pallas_call(
        own_kernel,
        out_shape=[rows, rows, sums, sums, sums],
        in_specs=[VMEM] * 3,
        out_specs=[VMEM] * 5,
        **params(count, token, 1),
    )(queries, other, own)
    return tuple(result[:2]), tuple(result[2:])


def attend(starts, rows, states, wanted, size_key, token, pack=False):
    count = rows[0].shape[0]
    items = []
    for _, mine in wanted:
        items += [item for item in mine if not any(item is other for other in items)]
    places = [
        (group, tuple(at for item in mine for at, other in enumerate(items) if other is item))
        for group, mine in wanted
    ]
    arrays, pieces = zip(*items)
    blocks = sum(array.shape[0] for array in arrays) // (2 * token)
    room = -(-blocks // STEP) * STEP * token
    fresh = tuple(group for group, _ in wanted if states[group] is None)
    sums = [jax.ShapeDtypeStruct((count, HD), jnp.float32)] * 3
    outs = sums * len(wanted)
    if pack:
        outs.append(jax.ShapeDtypeStruct((2 * count, HD), jnp.float32))
    operands = [starts, *(rows[group] for group, _ in wanted), *arrays]
    aliases = {}
    for at, (group, _) in enumerate(wanted):
        if group not in fresh:
            aliases.update({len(operands) + index: 3 * at + index for index in range(3)})
            operands += states[group]
    kernel = functools.partial(attend_kernel, pieces, places, fresh, pack, size_key, token)
    result = pl.pallas_call(
        kernel,
        out_shape=outs,
        in_specs=[SMEM] + [VMEM] * (len(operands) - 1),
        out_specs=[VMEM] * len(outs),
        input_output_aliases=aliases,
        scratch_shapes=[pltpu.VMEM((room, HD), jnp.bfloat16)] * 2,
        **params(count * len(wanted), token, blocks),
    )(*operands)
    states = list(states)
    for at, (group, _) in enumerate(wanted):
        states[group] = tuple(result[3 * at : 3 * at + 3])
    return states, result[-1]


def finish(sums, packed, shape):
    token, width = shape
    return pl.pallas_call(
        finish_kernel,
        out_shape=jax.ShapeDtypeStruct(shape, jnp.float32),
        in_specs=[VMEM] * 4,
        out_specs=VMEM,
        **params(width // HD * token, token, 1),
    )(*sums, packed)


def move(array, mask_even, mask_odd, place):
    size_query, size_key = lax.axis_size("pb"), lax.axis_size("ka")
    pairs = []
    for query in range(size_query):
        source = query ^ (mask_odd if query % 2 else mask_even)
        for key in range(size_key):
            pairs.append((source * size_key + (key ^ place), query * size_key + key))
    return lax.ppermute(array, AXES, pairs)


def stages(size_query):
    bits = [1 << at for at in range(1, size_query.bit_length() - 1)]
    return [bits[at : at + 2] for at in range(0, len(bits), 2)]


def paired(size_query, size_key):
    plan = stages(size_query)
    return len(plan) == 1 and len(plan[0]) == 2 and size_key > 1


def spread_near(item, bits):
    array, parts = item
    one, two = bits
    near = (move(array, one, two, 0), shifted(parts, one, two))
    side = (move(array, two, one, 0), shifted(parts, two, one))
    return near, side


def spread(item, bits):
    array, parts = item
    one, two = bits[0], bits[-1]
    near = (move(array, one, two, 0), shifted(parts, one, two))
    if one == two:
        return near, None, None
    side = (move(array, two, one, 0), shifted(parts, two, one))
    far = (move(near[0], two, one, 0), shifted(near[1], two, one))
    return near, side, far


def shifted(parts, even, odd):
    return tuple((at, number, base, one ^ even, two ^ odd) for at, number, base, one, two in parts)


def gathered_attention(queries, keys, values, positions):
    token = queries.shape[0]
    size_query, size_key = lax.axis_size("pb"), lax.axis_size("ka")
    assert size_query & (size_query - 1) == 0 and size_key & (size_key - 1) == 0 and size_query > 1
    starts = positions.reshape(-1, token)[:, 0]
    own = packed_blocks(keys, values)
    other = move(queries, 1, 1, 0)
    column = [own] + [move(own, 0, 0, place) for place in range(1, size_key)]
    half = max(size_key // 2, 1)
    held = [
        (jnp.concatenate(column[base : base + half], axis=0), ((0, half, base, 0, 0),))
        for base in range(0, size_key, half)
    ]

    rows, sums = attend_own(queries, other, own)
    plan = stages(size_query)
    if paired(size_query, size_key):
        (lower, upper), (one, two) = held, plan[0]
        near, side = spread_near(lower, (one, two))
        both = one ^ two
        far = (move(lower[0], both, both, 0), shifted(lower[1], both, both))
        near_up, side_up = spread_near(upper, (one, two))
        far_up = (move(upper[0], both, both, 0), shifted(upper[1], both, both))
        steps = [[(1, [lower])], [(0, [near, side, far, upper]), (1, [near, side, far, upper])], [(1, [near_up, side_up, far_up])]]
        rest = [lower, near_up, side_up, far_up]
    else:
        shared = [held]
        for bits in plan:
            more = [item for piece in held for item in spread(piece, bits) if item is not None]
            shared.append(more)
            held = held + more
        rest = shared.pop()
        steps = [[(0, group), (1, group)] for group in shared] + [[(1, rest)]]

    states = [sums, None]
    attend_to = functools.partial(attend, size_key=size_key, token=token)
    for number, wanted in enumerate(steps):
        pack = number == len(steps) - 1
        states, packed = attend_to(starts, rows, states, wanted, pack=pack)
    packed = move(packed, 1, 1, 0)
    states, _ = attend_to(starts, rows, states, [(0, rest)])
    return finish(states[0], packed, queries.shape)


def solution(mesh):
    return jax.shard_map(
        gathered_attention,
        mesh=mesh,
        in_specs=(P(AXES, None), P(AXES, None), P(AXES, None), P()),
        out_specs=P(AXES, None),
        check_vma=False,
    )
```

```python
import functools
import math

import jax
import jax.numpy as jnp
from jax import lax
from jax.experimental import pallas as pl
from jax.experimental.pallas import tpu as pltpu
from jax.sharding import PartitionSpec as P


HD = 128
AXES = ("pb", "ka")
BIG = -1e30
STEP = 4
LIMIT = 24 << 20

VMEM = pl.BlockSpec(memory_space=pltpu.VMEM)
SMEM = pl.BlockSpec(memory_space=pltpu.SMEM)


def combine(rows, keys, values, sums, to_log2, mask=None, skip_last=False):
    score = lax.dot_general(
        rows, keys, (((1,), (1,)), ((), ())), preferred_element_type=jnp.float32
    )
    if mask is not None:
        score = jnp.where(mask, score, BIG)
    parts = [score[:, at : at + HD] for at in range(0, keys.shape[0], HD)]
    if skip_last:
        parts[-1] = jnp.full_like(parts[-1], BIG)
    top = jnp.max(functools.reduce(jnp.maximum, parts), axis=1, keepdims=True)
    if sums is None:
        top = jnp.broadcast_to(top, (rows.shape[0], HD))
    else:
        top = jnp.maximum(sums[0], top)
    weights = [jnp.exp2((part - top) * to_log2) for part in parts]
    total = functools.reduce(jnp.add, weights)
    highs = [weight.astype(jnp.bfloat16) for weight in weights]
    lows = [
        (weight - high.astype(jnp.float32)).astype(jnp.bfloat16)
        for weight, high in zip(weights, highs)
    ]
    halves = [jnp.concatenate(half, axis=1) if len(half) > 1 else half[0] for half in (highs, lows)]
    over = (((1,), (0,)), ((), ()))
    if len(parts) < STEP:
        result = sum(
            lax.dot_general(half, values, over, preferred_element_type=jnp.float32)
            for half in halves
        )
    else:
        both = jnp.concatenate(halves, axis=0)
        result = lax.dot_general(both, values, over, preferred_element_type=jnp.float32)
        result = result[: rows.shape[0]] + result[rows.shape[0] :]
    if sums is None:
        return top, total, result
    largest, totals, summed = sums
    factor = jnp.exp2((largest - top) * to_log2)
    return top, totals * factor + total, summed * factor + result


TO_LOG2 = math.log2(math.e) / HD**0.5


def pack_kernel(keys_ref, values_ref, out_ref, done):
    token = keys_ref.shape[0]
    copies = [
        pltpu.make_async_copy(keys_ref, out_ref.at[:token, :], done.at[0]),
        pltpu.make_async_copy(values_ref, out_ref.at[token:, :], done.at[1]),
    ]
    for copy in copies:
        copy.start()
    for copy in copies:
        copy.wait()


def own_kernel(
    queries_ref, other_ref, own_ref, rows_ref, other_rows_ref, largest_ref, totals_ref, summed_ref
):
    token, width = queries_ref.shape
    heads = width // HD
    for head in range(heads):
        rows, columns = slice(head * token, (head + 1) * token), slice(head * HD, (head + 1) * HD)
        rows_ref[rows, :] = queries_ref[:, columns]
        other_rows_ref[rows, :] = other_ref[:, columns]
    shape = (heads, token, token)
    causal = lax.broadcasted_iota(jnp.int32, shape, 2) <= lax.broadcasted_iota(jnp.int32, shape, 1)
    keys, values = own_ref[:token, :], own_ref[token:, :]
    mask = causal.reshape(heads * token, token)
    new = combine(rows_ref[...], keys, values, None, TO_LOG2, mask)
    for held, value in zip((largest_ref, totals_ref, summed_ref), new):
        held[...] = value


def attend_kernel(pieces, groups, fresh, pack, size_key, token, *refs):
    refs = list(refs)
    take = lambda number: [refs.pop(0) for _ in range(number)]
    (starts_ref,) = take(1)
    rows_refs = take(len(groups))
    block_refs = take(len(pieces))
    take(3 * (len(groups) - len(fresh)))
    states = [take(3) for _ in groups]
    packed_refs = take(1 if pack else 0)
    keys_ref, values_ref = take(2)

    own_pb, own_ka = lax.axis_index("pb"), lax.axis_index("ka")
    core = own_pb % 2

    def compact(bound, places):
        seen = jnp.int32(0)
        for place in places:
            ref = block_refs[place]
            for offset, number, base, mask_even, mask_odd in pieces[place]:
                source = (own_pb ^ jnp.where(core == 0, mask_even, mask_odd)) * size_key
                for at in range(number):
                    visible = starts_ref[source + (own_ka ^ (base + at))] < bound
                    row = (offset + at) * 2 * token

                    @pl.when(visible)
                    def _():
                        target = pl.ds(pl.multiple_of(seen * token, token), token)
                        keys_ref[target, :] = ref[row : row + token, :]
                        values_ref[target, :] = ref[row + token : row + 2 * token, :]

                    seen = seen + visible.astype(jnp.int32)

        @pl.when(seen % STEP == STEP - 1)
        def _():
            target = pl.ds(pl.multiple_of(seen * token, token), token)
            keys_ref[target, :] = jnp.zeros((token, HD), keys_ref.dtype)
            values_ref[target, :] = jnp.zeros((token, HD), values_ref.dtype)

        return seen

    def attend_group(rows_ref, state, seen):
        def update(first, number, skip_last=False):
            part = pl.ds(pl.multiple_of(first * token, token), number * token)
            sums = [held[...] for held in state]
            new = combine(
                rows_ref[...],
                keys_ref[part, :],
                values_ref[part, :],
                sums,
                TO_LOG2,
                skip_last=skip_last,
            )
            for held, value in zip(state, new):
                held[...] = value

        def many(index, _):
            update(index * STEP, STEP)
            return 0

        full, left = seen // STEP, seen % STEP
        lax.fori_loop(0, full, many, 0)
        done = full * STEP
        pl.when(left == 1)(functools.partial(update, done, 1))
        pl.when(left == 2)(functools.partial(update, done, 2))
        pl.when(left == 3)(functools.partial(update, done, STEP, True))

    for (group, places), rows_ref, state in zip(groups, rows_refs, states):
        if group in fresh:
            state[0][...] = jnp.full_like(state[0], BIG)
            state[1][...] = jnp.zeros_like(state[1])
            state[2][...] = jnp.zeros_like(state[2])
        bound = starts_ref[(own_pb ^ group) * size_key + own_ka]
        attend_group(rows_ref, state, compact(bound, places))

    if pack:
        largest_ref, totals_ref, summed_ref = states[0]
        count = summed_ref.shape[0]
        lane = lax.broadcasted_iota(jnp.int32, (count, HD), 1)
        total = jnp.sum(totals_ref[...], axis=1, keepdims=True)
        packed_refs[0][:count, :] = summed_ref[...]
        packed_refs[0][count:, :] = jnp.where(lane < HD // 2, largest_ref[...], total)


def finish_kernel(largest_ref, totals_ref, summed_ref, packed_ref, out_ref):
    token, width = out_ref.shape
    count = summed_ref.shape[0]
    for head in range(width // HD):
        rows = slice(head * token, (head + 1) * token)
        packed = packed_ref[count + head * token : count + (head + 1) * token, :]
        largest = largest_ref[rows, :]
        other = packed[:, :1]
        top = jnp.maximum(largest, other)
        mine, theirs = jnp.exp2((largest - top) * TO_LOG2), jnp.exp2((other - top) * TO_LOG2)
        total = jnp.sum(totals_ref[rows, :], axis=1, keepdims=True) * mine
        total += packed[:, HD // 2 : HD // 2 + 1] * theirs
        summed = summed_ref[rows, :] * mine + packed_ref[rows, :] * theirs
        out_ref[:, head * HD : (head + 1) * HD] = summed / total


def params(rows, token, blocks):
    return dict(
        compiler_params=pltpu.CompilerParams(vmem_limit_bytes=LIMIT),
        cost_estimate=pl.CostEstimate(
            flops=6 * rows * HD * token * blocks,
            transcendentals=rows * token * blocks,
            bytes_accessed=1 << 20,
        ),
    )


def packed_blocks(keys, values):
    token, width = keys.shape
    return pl.pallas_call(
        pack_kernel,
        out_shape=jax.ShapeDtypeStruct((2 * token, width), keys.dtype),
        in_specs=[pl.BlockSpec(memory_space=pltpu.HBM)] * 2,
        out_specs=VMEM,
        scratch_shapes=[pltpu.SemaphoreType.DMA((2,))],
        compiler_params=pltpu.CompilerParams(vmem_limit_bytes=LIMIT),
    )(*(pltpu.with_memory_space_constraint(array, pltpu.HBM) for array in (keys, values)))


def attend_own(queries, other, own):
    token, width = queries.shape
    count = width // HD * token
    rows = jax.ShapeDtypeStruct((count, HD), jnp.bfloat16)
    sums = jax.ShapeDtypeStruct((count, HD), jnp.float32)
    result = pl.pallas_call(
        own_kernel,
        out_shape=[rows, rows, sums, sums, sums],
        in_specs=[VMEM] * 3,
        out_specs=[VMEM] * 5,
        **params(count, token, 1),
    )(queries, other, own)
    return tuple(result[:2]), tuple(result[2:])


def attend(starts, rows, states, wanted, size_key, token, pack=False):
    count = rows[0].shape[0]
    items = []
    for _, mine in wanted:
        items += [item for item in mine if not any(item is other for other in items)]
    places = [
        (group, tuple(at for item in mine for at, other in enumerate(items) if other is item))
        for group, mine in wanted
    ]
    arrays, pieces = zip(*items)
    blocks = sum(array.shape[0] for array in arrays) // (2 * token)
    room = -(-blocks // STEP) * STEP * token
    fresh = tuple(group for group, _ in wanted if states[group] is None)
    sums = [jax.ShapeDtypeStruct((count, HD), jnp.float32)] * 3
    outs = sums * len(wanted)
    if pack:
        outs.append(jax.ShapeDtypeStruct((2 * count, HD), jnp.float32))
    operands = [starts, *(rows[group] for group, _ in wanted), *arrays]
    aliases = {}
    for at, (group, _) in enumerate(wanted):
        if group not in fresh:
            aliases.update({len(operands) + index: 3 * at + index for index in range(3)})
            operands += states[group]
    kernel = functools.partial(attend_kernel, pieces, places, fresh, pack, size_key, token)
    result = pl.pallas_call(
        kernel,
        out_shape=outs,
        in_specs=[SMEM] + [VMEM] * (len(operands) - 1),
        out_specs=[VMEM] * len(outs),
        input_output_aliases=aliases,
        scratch_shapes=[pltpu.VMEM((room, HD), jnp.bfloat16)] * 2,
        **params(count * len(wanted), token, blocks),
    )(*operands)
    states = list(states)
    for at, (group, _) in enumerate(wanted):
        states[group] = tuple(result[3 * at : 3 * at + 3])
    return states, result[-1]


def finish(sums, packed, shape):
    token, width = shape
    return pl.pallas_call(
        finish_kernel,
        out_shape=jax.ShapeDtypeStruct(shape, jnp.float32),
        in_specs=[VMEM] * 4,
        out_specs=VMEM,
        **params(width // HD * token, token, 1),
    )(*sums, packed)


def move(array, mask_even, mask_odd, place):
    size_query, size_key = lax.axis_size("pb"), lax.axis_size("ka")
    pairs = []
    for query in range(size_query):
        source = query ^ (mask_odd if query % 2 else mask_even)
        for key in range(size_key):
            pairs.append((source * size_key + (key ^ place), query * size_key + key))
    return lax.ppermute(array, AXES, pairs)


def stages(size_query):
    bits = [1 << at for at in range(1, size_query.bit_length() - 1)]
    return [bits[at : at + 2] for at in range(0, len(bits), 2)]


def paired(size_query, size_key):
    plan = stages(size_query)
    return len(plan) == 1 and len(plan[0]) == 2 and size_key > 1


def spread_near(item, bits):
    array, parts = item
    one, two = bits
    near = (move(array, one, two, 0), shifted(parts, one, two))
    side = (move(array, two, one, 0), shifted(parts, two, one))
    return near, side


def spread(item, bits):
    array, parts = item
    one, two = bits[0], bits[-1]
    near = (move(array, one, two, 0), shifted(parts, one, two))
    if one == two:
        return near, None, None
    side = (move(array, two, one, 0), shifted(parts, two, one))
    far = (move(near[0], two, one, 0), shifted(near[1], two, one))
    return near, side, far


def shifted(parts, even, odd):
    return tuple((at, number, base, one ^ even, two ^ odd) for at, number, base, one, two in parts)


def gathered_attention(queries, keys, values, positions):
    token = queries.shape[0]
    size_query, size_key = lax.axis_size("pb"), lax.axis_size("ka")
    assert size_query & (size_query - 1) == 0 and size_key & (size_key - 1) == 0 and size_query > 1
    starts = positions.reshape(-1, token)[:, 0]
    own = packed_blocks(keys, values)
    other = move(queries, 1, 1, 0)
    column = [own] + [move(own, 0, 0, place) for place in range(1, size_key)]
    half = max(size_key // 2, 1)
    held = [
        (jnp.concatenate(column[base : base + half], axis=0), ((0, half, base, 0, 0),))
        for base in range(0, size_key, half)
    ]

    rows, sums = attend_own(queries, other, own)
    plan = stages(size_query)
    if paired(size_query, size_key):
        (lower, upper), (one, two) = held, plan[0]
        near, side = spread_near(lower, (one, two))
        both = one ^ two
        far = (move(lower[0], both, both, 0), shifted(lower[1], both, both))
        near_up, side_up = spread_near(upper, (one, two))
        far_up = (move(upper[0], both, both, 0), shifted(upper[1], both, both))
        steps = [[(0, [lower]), (1, [lower])], [(0, [near, side, far, upper]), (1, [near, side, far, upper])], [(1, [near_up, side_up, far_up])]]
        rest = [near_up, side_up, far_up]
    else:
        shared = [held]
        for bits in plan:
            more = [item for piece in held for item in spread(piece, bits) if item is not None]
            shared.append(more)
            held = held + more
        rest = shared.pop()
        steps = [[(0, group), (1, group)] for group in shared] + [[(1, rest)]]

    states = [sums, None]
    attend_to = functools.partial(attend, size_key=size_key, token=token)
    for number, wanted in enumerate(steps):
        pack = number == len(steps) - 1
        states, packed = attend_to(starts, rows, states, wanted, pack=pack)
    packed = move(packed, 1, 1, 0)
    states, _ = attend_to(starts, rows, states, [(0, rest)])
    return finish(states[0], packed, queries.shape)


def solution(mesh):
    return jax.shard_map(
        gathered_attention,
        mesh=mesh,
        in_specs=(P(AXES, None), P(AXES, None), P(AXES, None), P()),
        out_specs=P(AXES, None),
        check_vma=False,
    )
```
